512 devices in a mesh: ctx: 32 (over x, z_hi, core), head: 16 (over y, z_lo).
Axes of the slice: x: 4, y: 4, z: 16 (z_hi: 4, z_lo: 4; z = z_hi * 4 + z_lo), core: 2. Of those that a mesh axis runs over, the one named last changes fastest.
Arguments:
- query_states: bfloat16 [16384, 4096], P(('ctx', 'head')), may hold values from -6 to 6
- key_states: bfloat16 [16384, 2048], P(('ctx', 'head')), may hold values from -6 to 6
- value_states: bfloat16 [16384, 2048], P(('ctx', 'head')), may hold values from -6 to 6
- grad_out: bfloat16 [16384, 4096], P(('ctx', 'head')), may hold values from -6 to 6
- pack_table: int32 [8, 4], replicated, may hold values from 0 to 16384, as said below
Outputs:
- grad_query: bfloat16 [16384, 4096], P(('ctx', 'head'))
- grad_key: bfloat16 [16384, 2048], P(('ctx', 'head'))
- grad_value: bfloat16 [16384, 2048], P(('ctx', 'head'))
The draws below stay inside these ranges and needn't reach their ends.
Inputs may be any that keep to these rules, and one draw needn't show every extreme that they name: `pack_table`: one row a pack, in order of the stream: start, prompt end (the chosen response's start), rejected response's start, end. The packs tile 0 to 16384 without gaps; inner pack boundaries lie within 512 of the multiples of 2048. Each response has 128 to 512 tokens; some response has exactly 512, and with two or more packs some chosen and some rejected response both do.
All inputs are finite; a program needn't handle non-finite values.
Results may differ from the reference program's by a relative error of at most 0.006.
Values may be sent and summed in bfloat16 or wider, within the bound.
No kernel may reach another device: no remote copies, remote signals or barrier semaphores. Data moves between devices by JAX's collectives and lax.ppermute only.
A program may use at most 64 MiB of HBM per device.

```python
import jax
import jax.numpy as jnp
from jax import lax

HEAD_DIM = 128
GROUP_SIZE = 2
WINDOW = 4096
RESP_MOST = 512
PACK_MEAN = 2048
TOK_DEV = 512
KV_HEADS = 16
QUERY_HEADS = 32
TOKENS = 16384
PACKS = 8
REACH = 6
N_CTX = 32


def draw_pack_table(key, part):
    key_cut, key_chosen, key_reject, key_pick = jax.random.split(key, 4)
    inner_index = jnp.arange(1, PACKS, dtype=jnp.int32)
    jitter = jax.random.randint(key_cut, (PACKS - 1,), -(PACK_MEAN // 4), PACK_MEAN // 4 + 1, dtype=jnp.int32)
    inner = inner_index * PACK_MEAN + jitter
    starts = jnp.concatenate([jnp.zeros((1,), jnp.int32), inner])
    ends = jnp.concatenate([inner, jnp.full((1,), TOKENS, jnp.int32)])
    chosen_len = jax.random.randint(key_chosen, (PACKS,), RESP_MOST // 4, RESP_MOST + 1, dtype=jnp.int32)
    reject_len = jax.random.randint(key_reject, (PACKS,), RESP_MOST // 4, RESP_MOST + 1, dtype=jnp.int32)
    which_side = jax.random.randint(key_pick, (), 0, 2, dtype=jnp.int32)
    if PACKS > 1:
        chosen_len = chosen_len.at[0].set(RESP_MOST)
        reject_len = reject_len.at[PACKS - 1].set(RESP_MOST)
    else:
        chosen_len = chosen_len.at[0].set(jnp.where(which_side == 0, RESP_MOST, chosen_len[0]).astype(jnp.int32))
        reject_len = reject_len.at[0].set(jnp.where(which_side == 1, RESP_MOST, reject_len[0]).astype(jnp.int32))
    reject_start = ends - reject_len
    chosen_start = reject_start - chosen_len
    return jnp.stack([starts, chosen_start, reject_start, ends], axis=1).astype(jnp.int32)


def level_of(rng, extent, pieces, smallest, largest):
    level, own = 1.0, jax.random.fold_in(rng, 6)
    for dim, parts in pieces:
        steps = jnp.exp(jax.random.uniform(jax.random.fold_in(own, dim), (parts,), jnp.float32, smallest / len(pieces), largest / len(pieces)))
        level = level * jnp.repeat(steps, extent[dim] // parts).reshape([-1 if axis == dim else 1 for axis in range(len(extent))])
    return level


def noise(own_key, dims, deviation, most, cuts=(), held_as=jnp.bfloat16):
    loudness = level_of(own_key, dims, cuts, -0.22, 0.18) if cuts else 1.0
    values = jax.random.normal(own_key, dims, jnp.float32) * deviation * loudness
    return jnp.minimum(jnp.maximum(values, -most), most).astype(held_as)


def setup_inputs(seed: int = 0) -> dict:
    splits = jax.random.split(jax.random.key(seed), 6)
    return {
        "query_states": noise(splits[0], (TOKENS, QUERY_HEADS * HEAD_DIM), 1.0, 6.0, ((0, 512),)),
        "key_states": noise(splits[1], (TOKENS, KV_HEADS * HEAD_DIM), 1.0, 6.0, ((0, 512),)),
        "value_states": noise(splits[2], (TOKENS, KV_HEADS * HEAD_DIM), 1.0, 6.0, ((0, 512),)),
        "grad_out": noise(splits[3], (TOKENS, QUERY_HEADS * HEAD_DIM), 1.0, 6.0, ((0, 512),)),
        "pack_table": draw_pack_table(jax.random.fold_in(splits[5], 71), 0),
    }


soft_cap = 50.0
score_scale = 1.0 / 12.0


def round_half(values):
    return lax.optimization_barrier(values.astype(jnp.bfloat16)).astype(jnp.float32)


def token_info(positions, pack_table):
    inside = (positions[:, None] >= pack_table[None, :, 0]).astype(jnp.int32)
    pack_id = jnp.sum(inside, axis=1) - 1
    selected = (pack_id[:, None] == jnp.arange(PACKS, dtype=jnp.int32)[None, :]).astype(jnp.int32)
    bounds = jnp.sum(selected[:, :, None] * pack_table[None, :, :], axis=1)
    token_role = (positions >= bounds[:, 1]).astype(jnp.int32) + (positions >= bounds[:, 2]).astype(jnp.int32)
    logical = jnp.where(token_role == 2, positions - bounds[:, 2] + bounds[:, 1], positions) - bounds[:, 0]
    return pack_id, token_role, logical


def allowed(query_info, key_info):
    same_pack = query_info[0][:, None] == key_info[0][None, :]
    distance = query_info[2][:, None] - key_info[2][None, :]
    inside = (distance >= 0) & (distance < WINDOW)
    crossing = (query_info[1][:, None] + key_info[1][None, :]) == 3
    return same_pack & inside & jnp.logical_not(crossing)


def capped_of(query_block, key_block):
    raw_score = jnp.einsum("qhgd,khd->hgqk", query_block, key_block) * score_scale
    return soft_cap * jnp.tanh(raw_score / soft_cap)


def reference(query_states, key_states, value_states, grad_out, pack_table):
    query_all = query_states.astype(jnp.float32).reshape(TOKENS, KV_HEADS, GROUP_SIZE, HEAD_DIM)
    grad_all = grad_out.astype(jnp.float32).reshape(TOKENS, KV_HEADS, GROUP_SIZE, HEAD_DIM)
    key_all = key_states.astype(jnp.float32).reshape(TOKENS, KV_HEADS, HEAD_DIM)
    value_all = value_states.astype(jnp.float32).reshape(TOKENS, KV_HEADS, HEAD_DIM)
    local_rows = jnp.arange(TOK_DEV, dtype=jnp.int32)

    def shard_step(shard, carry):
        grad_q_all, grad_k_all, grad_v_all = carry
        shard = shard.astype(jnp.int32)
        first = shard * TOK_DEV
        query_block = lax.dynamic_slice_in_dim(query_all, first, TOK_DEV, 0)
        grad_block = lax.dynamic_slice_in_dim(grad_all, first, TOK_DEV, 0)
        query_info = token_info(first + local_rows, pack_table)
        row_total = jnp.zeros((KV_HEADS, GROUP_SIZE, TOK_DEV), jnp.float32)
        weighted = jnp.zeros((TOK_DEV, KV_HEADS, GROUP_SIZE, HEAD_DIM), jnp.float32)
        sources = []
        for offset in range(REACH + 1):
            source = shard - offset
            key_first = (jnp.maximum(source, 0) * TOK_DEV).astype(jnp.int32)
            key_block = lax.dynamic_slice_in_dim(key_all, key_first, TOK_DEV, 0)
            value_block = lax.dynamic_slice_in_dim(value_all, key_first, TOK_DEV, 0)
            visible = allowed(query_info, token_info(source * TOK_DEV + local_rows, pack_table))
            sources.append((key_first, key_block, value_block, visible))
            capped = capped_of(query_block, key_block)
            expo = jnp.where(visible[None, None], jnp.exp(capped), 0.0)
            row_total = row_total + jnp.sum(expo, axis=-1)
            weighted = weighted + jnp.einsum("hgqk,khd->qhgd", round_half(expo), value_block)
        attn_out = weighted / jnp.transpose(row_total, (2, 0, 1))[..., None]
        row_delta = jnp.sum(grad_block * attn_out, axis=-1)
        delta_heads = jnp.transpose(row_delta, (1, 2, 0))[..., None]
        grad_query_block = jnp.zeros((TOK_DEV, KV_HEADS, GROUP_SIZE, HEAD_DIM), jnp.float32)
        for offset in range(REACH + 1):
            key_first, key_block, value_block, visible = sources[offset]
            capped = capped_of(query_block, key_block)
            prob = jnp.where(visible[None, None], jnp.exp(capped), 0.0) / row_total[..., None]
            dprob = jnp.einsum("qhgd,khd->hgqk", grad_block, value_block)
            ratio = capped / soft_cap
            dscore = round_half(((prob * (dprob - delta_heads)) * (1.0 - ratio * ratio)) * score_scale)
            grad_query_block = grad_query_block + jnp.einsum("hgqk,khd->qhgd", dscore, key_block)
            part_key = jnp.einsum("hgqk,qhgd->khd", dscore, query_block)
            part_value = jnp.einsum("hgqk,qhgd->khd", round_half(prob), grad_block)
            old_key = lax.dynamic_slice_in_dim(grad_k_all, key_first, TOK_DEV, 0)
            grad_k_all = lax.dynamic_update_slice_in_dim(grad_k_all, old_key + part_key, key_first, 0)
            old_value = lax.dynamic_slice_in_dim(grad_v_all, key_first, TOK_DEV, 0)
            grad_v_all = lax.dynamic_update_slice_in_dim(grad_v_all, old_value + part_value, key_first, 0)
        grad_q_all = lax.dynamic_update_slice_in_dim(grad_q_all, grad_query_block, first, 0)
        return grad_q_all, grad_k_all, grad_v_all

    start_carry = (jnp.zeros((TOKENS, KV_HEADS, GROUP_SIZE, HEAD_DIM), jnp.float32),
                   jnp.zeros((TOKENS, KV_HEADS, HEAD_DIM), jnp.float32),
                   jnp.zeros((TOKENS, KV_HEADS, HEAD_DIM), jnp.float32))
    grad_q_all, grad_k_all, grad_v_all = lax.fori_loop(0, N_CTX, shard_step, start_carry)
    grad_query = grad_q_all.reshape(TOKENS, QUERY_HEADS * HEAD_DIM).astype(jnp.bfloat16)
    grad_key = grad_k_all.reshape(TOKENS, KV_HEADS * HEAD_DIM).astype(jnp.bfloat16)
    grad_value = grad_v_all.reshape(TOKENS, KV_HEADS * HEAD_DIM).astype(jnp.bfloat16)
    return (grad_query, grad_key, grad_value)
```

```python
import jax
import jax.numpy as jnp
from jax import lax
from jax.experimental import pallas as pl
from jax.experimental.pallas import tpu as pltpu
from jax.sharding import Mesh, PartitionSpec as P

HEAD_DIM = 128
WINDOW = 4096
SOFT_CAP = 50.0
SCORE_SCALE = 1.0 / 12.0

X, ZH, CORE, Y, ZL = 4, 4, 2, 4, 4
HEADS = ZH * ZL
SLAB = 4096
RUN = 128
HALO = 3
SLOTS = 2 * (HALO + ZH)
KB = 256
BLOCKS = SLOTS * 512 // KB
MOST = 14
PACK_STEP = 1 << 15


def token_codes(positions, pack_table):
    starts = pack_table[:, 0]
    pack_id = jnp.sum((positions[:, None] >= starts[None, :]).astype(jnp.int32), axis=1) - 1
    chosen = pack_id[:, None] == jnp.arange(pack_table.shape[0], dtype=jnp.int32)[None, :]
    bounds = jnp.sum(jnp.where(chosen[:, :, None], pack_table[None, :, :], 0), axis=1)
    role = (positions >= bounds[:, 1]).astype(jnp.int32) + (positions >= bounds[:, 2]).astype(
        jnp.int32
    )
    logical = (
        jnp.where(role == 2, positions - bounds[:, 2] + bounds[:, 1], positions) - bounds[:, 0]
    )
    return pack_id * PACK_STEP + logical, role, bounds[:, 0]


def attend(
    where_ref, query_code_ref, key_code_ref, qg_ref,
    own0, own1, own2, own3, own_other, halo0, halo1, halo2, halo3, halo_other,
    dq_ref, mine_ref, other_ref,
    keys, values, keys_t, values_t, ratios, expos, sums,
):
    y = where_ref[8]
    core = where_ref[9]
    f32, b16 = jnp.float32, jnp.bfloat16

    def place(slot, row, piece):
        block = slot * 2 + row // 2
        at = pl.multiple_of((row % 2) * RUN, RUN)
        keys[block, pl.ds(at, RUN), :] = piece[:, :HEAD_DIM]
        values[block, pl.ds(at, RUN), :] = piece[:, HEAD_DIM:]

    for dy, (own, halo) in enumerate(((own0, halo0), (own1, halo1), (own2, halo2), (own3, halo3))):
        row = (y + dy) % Y
        for c in range(ZH):
            place(2 * (HALO + c) + core, row, own[c * RUN : (c + 1) * RUN, :])
            place(2 * (HALO + c) + 1 - core, row, own_other[dy, c * RUN : (c + 1) * RUN, :])
        for c in range(HALO):
            place(2 * c + core, row, halo[c * RUN : (c + 1) * RUN, :])
            place(2 * c + 1 - core, row, halo_other[dy, c * RUN : (c + 1) * RUN, :])

    def prepare(block, carry):
        keys_t[block] = keys[block].T
        values_t[block] = values[block].T
        return carry

    lax.fori_loop(where_ref[0], BLOCKS, prepare, 0)

    def clear(block, carry):
        sums[block] = jnp.zeros((KB, 2 * HEAD_DIM), f32)
        return carry

    lax.fori_loop(0, BLOCKS, clear, 0)

    for c in range(ZH):
        rows = slice(c * RUN, (c + 1) * RUN)
        low = where_ref[c]
        high = where_ref[4 + c]
        query = jnp.concatenate([qg_ref[rows, 0:128], qg_ref[rows, 128:256]], axis=0)
        grad = jnp.concatenate([qg_ref[rows, 256:384], qg_ref[rows, 384:512]], axis=0)
        query_t = query.T
        grad_t = grad.T
        query_code = query_code_ref[c : c + 1, :]

        def forward(block, carry):
            total, weighted = carry
            raw = jnp.dot(keys[block], query_t, preferred_element_type=f32)
            ratio = jnp.tanh(raw * (SCORE_SCALE / SOFT_CAP))
            expo = jnp.exp(ratio * SOFT_CAP)
            gap = query_code - key_code_ref[pl.ds(pl.multiple_of(block * KB, KB), KB), :]
            seen = (gap >= 0) & (gap < 8 * WINDOW) & ((gap & 7) != 1)
            expo = jnp.concatenate(
                [jnp.where(seen, expo[:, :RUN], 0.0), jnp.where(seen, expo[:, RUN:], 0.0)], axis=1
            )
            ratios[block - low] = ratio
            expos[block - low] = expo
            total = total + jnp.sum(expo, axis=0, keepdims=True)
            weighted = weighted + jnp.dot(
                values_t[block], expo.astype(b16), preferred_element_type=f32
            )
            return total, weighted

        total, weighted = lax.fori_loop(
            low, high + 1, forward,
            (jnp.zeros((1, 2 * RUN), f32), jnp.zeros((HEAD_DIM, 2 * RUN), f32)),
        )
        scale = 1.0 / total
        delta = jnp.sum(grad_t.astype(f32) * weighted, axis=0, keepdims=True) * scale

        def backward(block, dq_t):
            ratio = ratios[block - low]
            prob = expos[block - low] * scale
            dprob = jnp.dot(values[block], grad_t, preferred_element_type=f32)
            dscore = prob * (dprob - delta) * ((1.0 - ratio * ratio) * SCORE_SCALE)
            dscore = dscore.astype(b16)
            dq_t = dq_t + jnp.dot(keys_t[block], dscore, preferred_element_type=f32)
            dk = jnp.dot(dscore, query, preferred_element_type=f32)
            dv = jnp.dot(prob.astype(b16), grad, preferred_element_type=f32)
            sums[block] = sums[block] + jnp.concatenate([dk, dv], axis=1)
            return dq_t

        dq_t = lax.fori_loop(low, high + 1, backward, jnp.zeros((HEAD_DIM, 2 * RUN), f32))
        dq_ref[rows, 0:128] = dq_t[:, :RUN].T.astype(b16)
        dq_ref[rows, 128:256] = dq_t[:, RUN:].T.astype(b16)

    for dy in range(Y):
        row = (y + dy) % Y
        at = pl.multiple_of((row % 2) * RUN, RUN)
        for c in range(HALO + ZH):
            mine_ref[dy, c * RUN : (c + 1) * RUN, :] = sums[
                (2 * c + core) * 2 + row // 2, pl.ds(at, RUN), :
            ]
            other_ref[dy, c * RUN : (c + 1) * RUN, :] = sums[
                (2 * c + 1 - core) * 2 + row // 2, pl.ds(at, RUN), :
            ].astype(b16)


def call_attend(where, query_code, key_code, qg, pieces):
    vmem = pl.BlockSpec(memory_space=pltpu.VMEM)
    rows = (HALO + ZH) * RUN
    return pl.pallas_call(
        attend,
        out_shape=(
            jax.ShapeDtypeStruct((ZH * RUN, 256), jnp.bfloat16),
            jax.ShapeDtypeStruct((Y, rows, 256), jnp.float32),
            jax.ShapeDtypeStruct((Y, rows, 256), jnp.bfloat16),
        ),
        in_specs=[pl.BlockSpec(memory_space=pltpu.SMEM)] + [vmem] * 13,
        out_specs=(vmem, vmem, vmem),
        scratch_shapes=[
            pltpu.VMEM((BLOCKS, KB, HEAD_DIM), jnp.bfloat16),
            pltpu.VMEM((BLOCKS, KB, HEAD_DIM), jnp.bfloat16),
            pltpu.VMEM((BLOCKS, HEAD_DIM, KB), jnp.bfloat16),
            pltpu.VMEM((BLOCKS, HEAD_DIM, KB), jnp.bfloat16),
            pltpu.VMEM((MOST, KB, 2 * RUN), jnp.float32),
            pltpu.VMEM((MOST, KB, 2 * RUN), jnp.float32),
            pltpu.VMEM((BLOCKS, KB, 2 * HEAD_DIM), jnp.float32),
        ],
        compiler_params=pltpu.CompilerParams(vmem_limit_bytes=56 << 20),
        name="attend",
    )(where, query_code, key_code, qg, *pieces)


def tables(x, core, y, pack_table):
    first = x * SLAB - HALO * 1024
    code, role, _ = token_codes(first + jnp.arange(SLOTS * 512, dtype=jnp.int32), pack_table)
    key_code = jnp.broadcast_to((8 * code + role)[:, None], (SLOTS * 512, RUN))
    runs = jnp.arange(ZH, dtype=jnp.int32)
    begin = x * SLAB + runs * 1024 + core * 512 + y * RUN
    position = (begin[:, None] + jnp.arange(RUN, dtype=jnp.int32)[None, :]).reshape(-1)
    code, role, start = token_codes(position, pack_table)
    query_code = (8 * code + 4 - role).reshape(ZH, RUN)
    high = (begin - first) // KB
    low = (start.reshape(ZH, RUN)[:, 0] - first) // KB
    low = jnp.maximum(jnp.maximum(low, high - (MOST - 1)), 0)
    where = jnp.concatenate([low, high, jnp.stack([y, core])])
    return where, query_code, key_code


def ring(size, by):
    return [(i, (i + by) % size) for i in range(size)]


def local(query_states, key_states, value_states, grad_out, pack_table):
    b16, f32 = jnp.bfloat16, jnp.float32
    x, core, y = lax.axis_index("x"), lax.axis_index("core"), lax.axis_index("y")
    z = ("zh", "zl")
    tokens = query_states.shape[0]

    def by_head(value):
        return jnp.transpose(value.reshape(tokens, HEADS, -1), (1, 0, 2))

    kv = jnp.concatenate([by_head(key_states), by_head(value_states)], axis=2)
    kv = lax.all_to_all(kv, z, split_axis=0, concat_axis=0, tiled=True).reshape(ZH * RUN, 256)
    qg = jnp.concatenate([by_head(query_states), by_head(grad_out)], axis=2)
    qg = lax.all_to_all(qg, z, split_axis=0, concat_axis=0, tiled=True).reshape(ZH * RUN, 512)
    where, query_code, key_code = tables(x, core, y, pack_table)

    halo = lax.ppermute(kv[RUN:], "x", [(i, i + 1) for i in range(X - 1)])
    own = [kv] + [lax.ppermute(kv, "y", ring(Y, -dy)) for dy in range(1, Y)]
    halos = [halo] + [lax.ppermute(halo, "y", ring(Y, -dy)) for dy in range(1, Y)]
    own_other = lax.ppermute(jnp.stack(own), "core", ring(CORE, 1))
    halo_other = lax.ppermute(jnp.stack(halos), "core", ring(CORE, 1))
    dq, mine, other = call_attend(
        where, query_code, key_code, qg, (*own, own_other, *halos, halo_other)
    )

    dq = lax.all_to_all(dq.reshape(HEADS, tokens, 256), z, split_axis=0, concat_axis=0, tiled=True)
    grad_query = jnp.transpose(dq, (1, 0, 2)).reshape(tokens, HEADS * 256)

    part = mine + lax.ppermute(other, "core", ring(CORE, 1)).astype(f32)
    total = part[0]
    for dy in range(1, Y):
        total = total + lax.ppermute(part[dy].astype(b16), "y", ring(Y, dy)).astype(f32)
    back = lax.ppermute(
        total[: HALO * RUN].astype(b16), "x", [(i + 1, i) for i in range(X - 1)]
    ).astype(f32)
    total = total[HALO * RUN :] + jnp.pad(back, ((RUN, 0), (0, 0)))
    dkv = lax.all_to_all(
        total.astype(b16).reshape(HEADS, tokens, 256), z, split_axis=0, concat_axis=0, tiled=True
    )
    dkv = jnp.transpose(dkv, (1, 0, 2))
    grad_key = dkv[:, :, :HEAD_DIM].reshape(tokens, HEADS * HEAD_DIM)
    grad_value = dkv[:, :, HEAD_DIM:].reshape(tokens, HEADS * HEAD_DIM)
    return grad_query, grad_key, grad_value


def solution(mesh):
    axes = ("x", "zh", "core", "y", "zl")
    fine = Mesh(mesh.devices.reshape(X, ZH, CORE, Y, ZL), axes)
    spread = P(axes, None)
    return jax.shard_map(
        local,
        mesh=fine,
        in_specs=(spread, spread, spread, spread, P()),
        out_specs=(spread, spread, spread),
        check_vma=False,
    )
```

```python
import jax
import jax.numpy as jnp
from jax import lax
from jax.experimental import pallas as pl
from jax.experimental.pallas import tpu as pltpu
from jax.sharding import Mesh, PartitionSpec as P

HEAD_DIM = 128
WINDOW = 4096
SOFT_CAP = 50.0
SCORE_SCALE = 1.0 / 12.0
LOG2_E = 1.4426950408889634

X, ZH, CORE, Y, ZL = 4, 4, 2, 4, 4
HEADS = ZH * ZL
SLAB = 4096
RUN = 128
RUNS = ZH + 1
SLOTS = 2 * RUNS
KB = 256
BLOCKS = SLOTS * 512 // KB
MOST = 14
PACK_STEP = 1 << 15


def token_codes(positions, pack_table):
    starts = pack_table[:, 0]
    pack_id = jnp.sum((positions[:, None] >= starts[None, :]).astype(jnp.int32), axis=1) - 1
    chosen = pack_id[:, None] == jnp.arange(pack_table.shape[0], dtype=jnp.int32)[None, :]
    bounds = jnp.sum(jnp.where(chosen[:, :, None], pack_table[None, :, :], 0), axis=1)
    role = (positions >= bounds[:, 1]).astype(jnp.int32) + (positions >= bounds[:, 2]).astype(
        jnp.int32
    )
    logical = (
        jnp.where(role == 2, positions - bounds[:, 2] + bounds[:, 1], positions) - bounds[:, 0]
    )
    return pack_id, logical, role, bounds[:, 0]


def by_two(low, stop, step, carry):
    pairs = (stop - low) // 2

    def both(i, carry):
        return step(low + 2 * i + 1, step(low + 2 * i, carry))

    carry = lax.fori_loop(0, pairs, both, carry)
    return lax.fori_loop(low + 2 * pairs, stop, step, carry)


def attend(
    where_ref, query_code_ref, key_code_ref, qg_ref, tail_ref,
    five0, five1, five2, five3, other_five,
    dq_ref, mine_ref, other_ref,
    keys, values, keys_t, values_t, ratios, expos, sums,
):
    y = where_ref[2 * RUNS]
    core = where_ref[2 * RUNS + 1]
    f32, b16 = jnp.float32, jnp.bfloat16

    def slot_of(run, side):
        return 2 * run + 1 + side if run < ZH else 9 * (1 - side)

    def place(slot, row, piece):
        block = slot * 2 + row // 2
        at = pl.multiple_of((row % 2) * RUN, RUN)
        keys[block, pl.ds(at, RUN), :] = piece[:, :HEAD_DIM]
        values[block, pl.ds(at, RUN), :] = piece[:, HEAD_DIM:]

    for dy, five in enumerate((five0, five1, five2, five3)):
        row = (y + dy) % Y
        for run in range(RUNS):
            rows = slice(run * RUN, (run + 1) * RUN)
            place(slot_of(run, core), row, five[rows, :])
            place(slot_of(run, 1 - core), row, other_five[dy, rows, :])

    for block in range(BLOCKS):
        keys_t[block] = keys[block].T
        values_t[block] = values[block].T
        sums[block] = jnp.zeros((KB, 2 * HEAD_DIM), f32)

    def one_run(run, source, rows):
        low = where_ref[run]
        high = where_ref[RUNS + run]
        query = jnp.concatenate([source[rows, 0:128], source[rows, 128:256]], axis=0)
        grad = jnp.concatenate([source[rows, 256:384], source[rows, 384:512]], axis=0)
        query_t = query.T
        grad_t = grad.T
        query_code = query_code_ref[run : run + 1, :]

        def forward(block, carry):
            total, weighted = carry
            raw = jnp.dot(keys[block], query_t, preferred_element_type=f32)
            ratio = jnp.tanh(raw * (SCORE_SCALE / SOFT_CAP))
            expo = jnp.exp2(ratio * (SOFT_CAP * LOG2_E))
            gap = query_code - key_code_ref[pl.ds(pl.multiple_of(block * KB, KB), KB), :]
            seen = (gap >= 0) & (gap < 8 * WINDOW) & ((gap & 7) != 1)
            expo = jnp.concatenate(
                [jnp.where(seen, expo[:, :RUN], 0.0), jnp.where(seen, expo[:, RUN:], 0.0)], axis=1
            )
            ratios[block - low] = ratio
            expos[block - low] = expo
            total = total + jnp.sum(expo, axis=0, keepdims=True)
            weighted = weighted + jnp.dot(
                values_t[block], expo.astype(b16), preferred_element_type=f32
            )
            return total, weighted

        total, weighted = by_two(
            low, high + 1, forward,
            (jnp.zeros((1, 2 * RUN), f32), jnp.zeros((HEAD_DIM, 2 * RUN), f32)),
        )
        scale = jnp.where(total > 0.0, 1.0 / total, 0.0)
        delta = jnp.sum(grad_t.astype(f32) * weighted, axis=0, keepdims=True) * scale

        def backward(block, dq_t):
            ratio = ratios[block - low]
            prob = expos[block - low] * scale
            dprob = jnp.dot(values[block], grad_t, preferred_element_type=f32)
            dscore = prob * (dprob - delta) * ((1.0 - ratio * ratio) * SCORE_SCALE)
            dscore = dscore.astype(b16)
            dq_t = dq_t + jnp.dot(keys_t[block], dscore, preferred_element_type=f32)
            dk = jnp.dot(dscore, query, preferred_element_type=f32)
            dv = jnp.dot(prob.astype(b16), grad, preferred_element_type=f32)
            sums[block] = sums[block] + jnp.concatenate([dk, dv], axis=1)
            return dq_t

        dq_t = by_two(low, high + 1, backward, jnp.zeros((HEAD_DIM, 2 * RUN), f32))
        out = slice(run * RUN, (run + 1) * RUN)
        dq_ref[out, 0:128] = dq_t[:, :RUN].T.astype(b16)
        dq_ref[out, 128:256] = dq_t[:, RUN:].T.astype(b16)

    for run in range(ZH):
        one_run(run, qg_ref, slice(run * RUN, (run + 1) * RUN))

    @pl.when(core == 0)
    def _():
        one_run(ZH, tail_ref, slice(0, RUN))

    @pl.when(core != 0)
    def _():
        dq_ref[ZH * RUN :, :] = jnp.zeros((RUN, 256), b16)

    for dy in range(Y):
        row = (y + dy) % Y
        at = pl.multiple_of((row % 2) * RUN, RUN)
        for run in range(RUNS):
            rows = slice(run * RUN, (run + 1) * RUN)
            mine_ref[dy, rows, :] = sums[slot_of(run, core) * 2 + row // 2, pl.ds(at, RUN), :]
            other_ref[dy, rows, :] = sums[
                slot_of(run, 1 - core) * 2 + row // 2, pl.ds(at, RUN), :
            ].astype(b16)


def call_attend(where, query_code, key_code, qg, tail, pieces):
    vmem = pl.BlockSpec(memory_space=pltpu.VMEM)
    rows = RUNS * RUN
    return pl.pallas_call(
        attend,
        out_shape=(
            jax.ShapeDtypeStruct((rows, 256), jnp.bfloat16),
            jax.ShapeDtypeStruct((Y, rows, 256), jnp.float32),
            jax.ShapeDtypeStruct((Y, rows, 256), jnp.bfloat16),
        ),
        in_specs=[pl.BlockSpec(memory_space=pltpu.SMEM)] + [vmem] * 9,
        out_specs=(vmem, vmem, vmem),
        scratch_shapes=[
            pltpu.VMEM((BLOCKS, KB, HEAD_DIM), jnp.bfloat16),
            pltpu.VMEM((BLOCKS, KB, HEAD_DIM), jnp.bfloat16),
            pltpu.VMEM((BLOCKS, HEAD_DIM, KB), jnp.bfloat16),
            pltpu.VMEM((BLOCKS, HEAD_DIM, KB), jnp.bfloat16),
            pltpu.VMEM((MOST, KB, 2 * RUN), jnp.float32),
            pltpu.VMEM((MOST, KB, 2 * RUN), jnp.float32),
            pltpu.VMEM((BLOCKS, KB, 2 * HEAD_DIM), jnp.float32),
        ],
        compiler_params=pltpu.CompilerParams(vmem_limit_bytes=50 << 20),
        name="attend",
    )(where, query_code, key_code, qg, tail, *pieces)


def tables(x, core, y, pack_table):
    first = x * SLAB - 512
    pack, logical, role, _ = token_codes(
        first + jnp.arange(SLOTS * 512, dtype=jnp.int32), pack_table
    )
    key_code = jnp.broadcast_to(
        (8 * (pack * PACK_STEP + logical) + role)[:, None], (SLOTS * 512, RUN)
    )
    runs = jnp.arange(RUNS, dtype=jnp.int32)
    tail = runs == ZH
    begin = x * SLAB + runs * 1024 + jnp.where(tail, 0, core * 512) + y * RUN
    position = begin[:, None] + jnp.arange(RUN, dtype=jnp.int32)[None, :]
    pack, logical, role, start = (
        part.reshape(RUNS, RUN) for part in token_codes(position.reshape(-1), pack_table)
    )
    home = pack // 2
    taken = jnp.where(tail[:, None], (home == x) & (core == 0), home >= x)
    taken = taken & (position < pack_table[-1, 3])
    query_code = jnp.where(taken, 8 * (pack * PACK_STEP + logical) + 4 - role, -(1 << 30))
    high = (begin - first) // KB
    low = (jnp.min(jnp.where(taken, start, 1 << 28), axis=1) - first) // KB
    low = jnp.maximum(jnp.maximum(low, high - (MOST - 1)), 0)
    some = jnp.any(taken, axis=1)
    low, high = jnp.where(some, low, 1), jnp.where(some, high, 0)
    where = jnp.concatenate([low, high, jnp.stack([y, core])])
    return where, query_code, key_code


def ring(size, by):
    return [(i, (i + by) % size) for i in range(size)]


def local(query_states, key_states, value_states, grad_out, pack_table):
    b16, f32 = jnp.bfloat16, jnp.float32
    x, core, y = lax.axis_index("x"), lax.axis_index("core"), lax.axis_index("y")
    z = ("zh", "zl")
    tokens = query_states.shape[0]
    borders = [(2 * i, 2 * i - 2) for i in range(1, X)] + [
        (2 * i + 1, 2 * i + 3) for i in range(X - 1)
    ]
    back = [(b, a) for a, b in borders]
    tails = [(2 * i, 2 * i - 2) for i in range(1, X)]

    def by_head(value):
        return jnp.transpose(value.reshape(tokens, HEADS, -1), (1, 0, 2))

    kv = jnp.concatenate([by_head(key_states), by_head(value_states)], axis=2)
    kv = lax.all_to_all(kv, z, split_axis=0, concat_axis=0, tiled=True).reshape(ZH * RUN, 256)
    qg = jnp.concatenate([by_head(query_states), by_head(grad_out)], axis=2)
    where, query_code, key_code = tables(x, core, y, pack_table)
    qg, where, query_code, key_code = lax.optimization_barrier((qg, where, query_code, key_code))
    qg = lax.all_to_all(qg, z, split_axis=0, concat_axis=0, tiled=True).reshape(ZH * RUN, 512)

    border = lax.dynamic_slice(kv, (core * (ZH - 1) * RUN, 0), (RUN, 256))
    border = lax.ppermute(border, ("x", "core"), borders)
    five = jnp.concatenate([kv, border], axis=0)
    fives = [five] + [lax.ppermute(five, "y", ring(Y, -dy)) for dy in range(1, Y)]
    other_five = lax.ppermute(jnp.stack(fives), "core", ring(CORE, 1))
    tail = lax.ppermute(qg[:RUN], ("x", "core"), tails)
    dq, mine, other = call_attend(
        where, query_code, key_code, qg, tail, (*fives, other_five)
    )

    dq_tail = lax.ppermute(dq[ZH * RUN :], ("x", "core"), [(b, a) for a, b in tails])
    dq = jnp.concatenate(
        [(dq[:RUN].astype(f32) + dq_tail.astype(f32)).astype(b16), dq[RUN : ZH * RUN]], axis=0
    )
    dq = lax.all_to_all(dq.reshape(HEADS, tokens, 256), z, split_axis=0, concat_axis=0, tiled=True)
    grad_query = jnp.transpose(dq, (1, 0, 2)).reshape(tokens, HEADS * 256)

    part = mine + lax.ppermute(other, "core", ring(CORE, 1)).astype(f32)
    total = part[0]
    for dy in range(1, Y):
        total = total + lax.ppermute(part[dy].astype(b16), "y", ring(Y, dy)).astype(f32)
    border = lax.ppermute(total[ZH * RUN :].astype(b16), ("x", "core"), back).astype(f32)
    gap = (ZH - 1) * RUN
    total = total[: ZH * RUN] + jnp.where(
        core == 0, jnp.pad(border, ((0, gap), (0, 0))), jnp.pad(border, ((gap, 0), (0, 0)))
    )
    dkv = lax.all_to_all(
        total.astype(b16).reshape(HEADS, tokens, 256), z, split_axis=0, concat_axis=0, tiled=True
    )
    dkv = jnp.transpose(dkv, (1, 0, 2))
    grad_key = dkv[:, :, :HEAD_DIM].reshape(tokens, HEADS * HEAD_DIM)
    grad_value = dkv[:, :, HEAD_DIM:].reshape(tokens, HEADS * HEAD_DIM)
    return grad_query, grad_key, grad_value


def solution(mesh):
    axes = ("x", "zh", "core", "y", "zl")
    fine = Mesh(mesh.devices.reshape(X, ZH, CORE, Y, ZL), axes)
    spread = P(axes, None)
    return jax.shard_map(
        local,
        mesh=fine,
        in_specs=(spread, spread, spread, spread, P()),
        out_specs=(spread, spread, spread),
        check_vma=False,
    )
```

```python
import jax
import jax.numpy as jnp
from jax import lax
from jax.experimental import pallas as pl
from jax.experimental.pallas import tpu as pltpu
from jax.sharding import Mesh, PartitionSpec as P

HEAD_DIM = 128
WINDOW = 4096
SOFT_CAP = 50.0
SCORE_SCALE = 1.0 / 12.0
LOG2_E = 1.4426950408889634

X, ZH, CORE, Y, ZL = 4, 4, 2, 4, 4
HEADS = ZH * ZL
SLAB = 4096
RUN = 128
RUNS = ZH + 1
SLOTS = 2 * RUNS
KB = 256
BLOCKS = SLOTS * 512 // KB
MOST = 14
PACK_STEP = 1 << 15


def token_codes(positions, pack_table):
    starts = pack_table[:, 0]
    pack_id = jnp.sum((positions[:, None] >= starts[None, :]).astype(jnp.int32), axis=1) - 1
    chosen = pack_id[:, None] == jnp.arange(pack_table.shape[0], dtype=jnp.int32)[None, :]
    bounds = jnp.sum(jnp.where(chosen[:, :, None], pack_table[None, :, :], 0), axis=1)
    role = (positions >= bounds[:, 1]).astype(jnp.int32) + (positions >= bounds[:, 2]).astype(
        jnp.int32
    )
    logical = (
        jnp.where(role == 2, positions - bounds[:, 2] + bounds[:, 1], positions) - bounds[:, 0]
    )
    return pack_id, logical, role, bounds[:, 0]


def by_two(low, stop, step, carry):
    pairs = (stop - low) // 2

    def both(i, carry):
        return step(low + 2 * i + 1, step(low + 2 * i, carry))

    carry = lax.fori_loop(0, pairs, both, carry)
    return lax.fori_loop(low + 2 * pairs, stop, step, carry)


def slot_of(run, side):
    return 2 * run + 1 + side if run < ZH else 9 * (1 - side)


def arrange(
    where_ref, five0, five1, five2, five3, other_five, keys, values, keys_t, values_t
):
    y = where_ref[2 * RUNS]
    core = where_ref[2 * RUNS + 1]

    def place(slot, row, piece):
        block = slot * 2 + row // 2
        at = pl.multiple_of((row % 2) * RUN, RUN)
        keys[block, pl.ds(at, RUN), :] = piece[:, :HEAD_DIM]
        values[block, pl.ds(at, RUN), :] = piece[:, HEAD_DIM:]

    for dy, five in enumerate((five0, five1, five2, five3)):
        row = (y + dy) % Y
        for run in range(RUNS):
            rows = slice(run * RUN, (run + 1) * RUN)
            place(slot_of(run, core), row, five[rows, :])
            place(slot_of(run, 1 - core), row, other_five[dy, rows, :])

    for block in range(BLOCKS):
        keys_t[block] = keys[block].T
        values_t[block] = values[block].T


def attend(
    where_ref, query_code_ref, key_code_ref, qg_ref, tail_ref, keys, values, keys_t, values_t,
    dq_ref, mine_ref, other_ref,
    ratios, expos, sums,
):
    y = where_ref[2 * RUNS]
    core = where_ref[2 * RUNS + 1]
    f32, b16 = jnp.float32, jnp.bfloat16

    for block in range(BLOCKS):
        sums[block] = jnp.zeros((KB, 2 * HEAD_DIM), f32)

    def one_run(run, source, rows):
        low = where_ref[run]
        high = where_ref[RUNS + run]
        query = jnp.concatenate([source[rows, 0:128], source[rows, 128:256]], axis=0)
        grad = jnp.concatenate([source[rows, 256:384], source[rows, 384:512]], axis=0)
        query_t = query.T
        grad_t = grad.T
        query_code = query_code_ref[run : run + 1, :]

        def forward(block, carry):
            total, weighted = carry
            raw = jnp.dot(keys[block], query_t, preferred_element_type=f32)
            ratio = jnp.tanh(raw * (SCORE_SCALE / SOFT_CAP))
            expo = jnp.exp2(ratio * (SOFT_CAP * LOG2_E))
            gap = query_code - key_code_ref[pl.ds(pl.multiple_of(block * KB, KB), KB), :]
            seen = (gap >= 0) & (gap < 8 * WINDOW) & ((gap & 7) != 1)
            expo = jnp.concatenate(
                [jnp.where(seen, expo[:, :RUN], 0.0), jnp.where(seen, expo[:, RUN:], 0.0)], axis=1
            )
            ratios[block - low] = ratio
            expos[block - low] = expo
            total = total + jnp.sum(expo, axis=0, keepdims=True)
            weighted = weighted + jnp.dot(
                values_t[block], expo.astype(b16), preferred_element_type=f32
            )
            return total, weighted

        total, weighted = by_two(
            low, high + 1, forward,
            (jnp.zeros((1, 2 * RUN), f32), jnp.zeros((HEAD_DIM, 2 * RUN), f32)),
        )
        scale = jnp.where(total > 0.0, 1.0 / total, 0.0)
        delta = jnp.sum(grad_t.astype(f32) * weighted, axis=0, keepdims=True) * scale

        def backward(block, dq_t):
            ratio = ratios[block - low]
            prob = expos[block - low] * scale
            dprob = jnp.dot(values[block], grad_t, preferred_element_type=f32)
            dscore = prob * (dprob - delta) * ((1.0 - ratio * ratio) * SCORE_SCALE)
            dscore = dscore.astype(b16)
            dq_t = dq_t + jnp.dot(keys_t[block], dscore, preferred_element_type=f32)
            dk = jnp.dot(dscore, query, preferred_element_type=f32)
            dv = jnp.dot(prob.astype(b16), grad, preferred_element_type=f32)
            sums[block] = sums[block] + jnp.concatenate([dk, dv], axis=1)
            return dq_t

        dq_t = by_two(low, high + 1, backward, jnp.zeros((HEAD_DIM, 2 * RUN), f32))
        out = slice(run * RUN, (run + 1) * RUN)
        dq_ref[out, 0:128] = dq_t[:, :RUN].T.astype(b16)
        dq_ref[out, 128:256] = dq_t[:, RUN:].T.astype(b16)

    for run in range(ZH):
        one_run(run, qg_ref, slice(run * RUN, (run + 1) * RUN))

    @pl.when(core == 0)
    def _():
        one_run(ZH, tail_ref, slice(0, RUN))

    @pl.when(core != 0)
    def _():
        dq_ref[ZH * RUN :, :] = jnp.zeros((RUN, 256), b16)

    for dy in range(Y):
        row = (y + dy) % Y
        at = pl.multiple_of((row % 2) * RUN, RUN)
        for run in range(RUNS):
            rows = slice(run * RUN, (run + 1) * RUN)
            mine_ref[dy, rows, :] = sums[slot_of(run, core) * 2 + row // 2, pl.ds(at, RUN), :]
            other_ref[dy, rows, :] = sums[
                slot_of(run, 1 - core) * 2 + row // 2, pl.ds(at, RUN), :
            ].astype(b16)


def call_arrange(where, pieces):
    vmem = pl.BlockSpec(memory_space=pltpu.VMEM)
    straight = jax.ShapeDtypeStruct((BLOCKS, KB, HEAD_DIM), jnp.bfloat16)
    turned = jax.ShapeDtypeStruct((BLOCKS, HEAD_DIM, KB), jnp.bfloat16)
    return pl.pallas_call(
        arrange,
        out_shape=(straight, straight, turned, turned),
        in_specs=[pl.BlockSpec(memory_space=pltpu.SMEM)] + [vmem] * 5,
        out_specs=(vmem,) * 4,
        compiler_params=pltpu.CompilerParams(vmem_limit_bytes=12 << 20),
        name="arrange",
    )(where, *pieces)


def call_attend(where, query_code, key_code, qg, tail, arranged):
    vmem = pl.BlockSpec(memory_space=pltpu.VMEM)
    rows = RUNS * RUN
    return pl.pallas_call(
        attend,
        out_shape=(
            jax.ShapeDtypeStruct((rows, 256), jnp.bfloat16),
            jax.ShapeDtypeStruct((Y, rows, 256), jnp.float32),
            jax.ShapeDtypeStruct((Y, rows, 256), jnp.bfloat16),
        ),
        in_specs=[pl.BlockSpec(memory_space=pltpu.SMEM)] + [vmem] * 8,
        out_specs=(vmem, vmem, vmem),
        scratch_shapes=[
            pltpu.VMEM((MOST, KB, 2 * RUN), jnp.float32),
            pltpu.VMEM((MOST, KB, 2 * RUN), jnp.float32),
            pltpu.VMEM((BLOCKS, KB, 2 * HEAD_DIM), jnp.float32),
        ],
        compiler_params=pltpu.CompilerParams(vmem_limit_bytes=32 << 20),
        name="attend",
    )(where, query_code, key_code, qg, tail, *arranged)


def tables(x, core, y, pack_table):
    first = x * SLAB - 512
    pack, logical, role, _ = token_codes(
        first + jnp.arange(SLOTS * 512, dtype=jnp.int32), pack_table
    )
    key_code = 8 * (pack * PACK_STEP + logical) + role
    key_code = jnp.broadcast_to(key_code[:, None], (SLOTS * 512, RUN))
    runs = jnp.arange(RUNS, dtype=jnp.int32)
    tail = runs == ZH
    begin = x * SLAB + runs * 1024 + jnp.where(tail, 0, core * 512) + y * RUN
    position = begin[:, None] + jnp.arange(RUN, dtype=jnp.int32)[None, :]
    pack, logical, role, start = (
        part.reshape(RUNS, RUN) for part in token_codes(position.reshape(-1), pack_table)
    )
    home = pack // 2
    taken = jnp.where(tail[:, None], (home == x) & (core == 0), home >= x)
    taken = taken & (position < pack_table[-1, 3])
    query_code = jnp.where(taken, 8 * (pack * PACK_STEP + logical) + 4 - role, -(1 << 30))
    high = (begin - first) // KB
    low = (jnp.min(jnp.where(taken, start, 1 << 28), axis=1) - first) // KB
    low = jnp.maximum(jnp.maximum(low, high - (MOST - 1)), 0)
    some = jnp.any(taken, axis=1)
    low, high = jnp.where(some, low, 1), jnp.where(some, high, 0)
    where = jnp.concatenate([low, high, jnp.stack([y, core])])
    return where, query_code, key_code


def ring(size, by):
    return [(i, (i + by) % size) for i in range(size)]


def local(query_states, key_states, value_states, grad_out, pack_table):
    b16, f32 = jnp.bfloat16, jnp.float32
    x, core, y = lax.axis_index("x"), lax.axis_index("core"), lax.axis_index("y")
    z = ("zh", "zl")
    tokens = query_states.shape[0]
    borders = [(2 * i, 2 * i - 2) for i in range(1, X)] + [
        (2 * i + 1, 2 * i + 3) for i in range(X - 1)
    ]
    back = [(b, a) for a, b in borders]
    tails = [(2 * i, 2 * i - 2) for i in range(1, X)]

    def by_head(value):
        return jnp.transpose(value.reshape(tokens, HEADS, -1), (1, 0, 2))

    kv = jnp.concatenate([by_head(key_states), by_head(value_states)], axis=2)
    qg = jnp.concatenate([by_head(query_states), by_head(grad_out)], axis=2)
    kv = lax.all_to_all(kv, z, split_axis=0, concat_axis=0, tiled=True)
    kv = kv.reshape(ZH * RUN, 256)
    where, query_code, key_code = tables(x, core, y, pack_table)
    qg, where, query_code, key_code = lax.optimization_barrier((qg, where, query_code, key_code))
    qg = lax.all_to_all(qg, z, split_axis=0, concat_axis=0, tiled=True)
    qg = qg.reshape(ZH * RUN, 512)

    border = lax.dynamic_slice(kv, (core * (ZH - 1) * RUN, 0), (RUN, 256))
    border = lax.ppermute(border, ("x", "core"), borders)
    five = jnp.concatenate([kv, border], axis=0)
    fives = [five] + [lax.ppermute(five, "y", ring(Y, -dy)) for dy in range(1, Y)]
    stack = jnp.stack(fives)
    other_five = lax.ppermute(stack, "core", ring(CORE, 1))
    arranged = call_arrange(where, (*fives, other_five))
    tail = lax.ppermute(qg[:RUN], ("x", "core"), tails)
    dq, mine, other = call_attend(where, query_code, key_code, qg, tail, arranged)

    other = lax.ppermute(other, "core", ring(CORE, 1))
    dq_tail = lax.ppermute(dq[ZH * RUN :], ("x", "core"), [(b, a) for a, b in tails])
    dq = jnp.concatenate(
        [(dq[:RUN].astype(f32) + dq_tail.astype(f32)).astype(b16), dq[RUN : ZH * RUN]], axis=0
    )
    dq = dq.reshape(HEADS, tokens, 256)
    dq = lax.all_to_all(dq, z, split_axis=0, concat_axis=0, tiled=True)
    grad_query = jnp.transpose(dq, (1, 0, 2)).reshape(tokens, HEADS * 256)

    part = mine + other.astype(f32)
    total = part[0]
    for dy in range(1, Y):
        total = total + lax.ppermute(part[dy].astype(b16), "y", ring(Y, dy)).astype(f32)
    border = lax.ppermute(total[ZH * RUN :].astype(b16), ("x", "core"), back).astype(f32)
    gap = (ZH - 1) * RUN
    total = total[: ZH * RUN] + jnp.where(
        core == 0, jnp.pad(border, ((0, gap), (0, 0))), jnp.pad(border, ((gap, 0), (0, 0)))
    )
    dkv = total.astype(b16).reshape(HEADS, tokens, 256)
    dkv = lax.all_to_all(dkv, z, split_axis=0, concat_axis=0, tiled=True)
    dkv = jnp.transpose(dkv, (1, 0, 2))
    grad_key = dkv[:, :, :HEAD_DIM].reshape(tokens, HEADS * HEAD_DIM)
    grad_value = dkv[:, :, HEAD_DIM:].reshape(tokens, HEADS * HEAD_DIM)
    return grad_query, grad_key, grad_value


def solution(mesh):
    axes = ("x", "zh", "core", "y", "zl")
    fine = Mesh(mesh.devices.reshape(X, ZH, CORE, Y, ZL), axes)
    spread = P(axes, None)
    return jax.shard_map(
        local,
        mesh=fine,
        in_specs=(spread, spread, spread, spread, P()),
        out_specs=(spread, spread, spread),
        check_vma=False,
    )
```

```python
import jax
import jax.numpy as jnp
from jax import lax
from jax.experimental import pallas as pl
from jax.experimental.pallas import tpu as pltpu
from jax.sharding import Mesh, PartitionSpec as P

HEAD_DIM = 128
WINDOW = 4096
SOFT_CAP = 50.0
SCORE_SCALE = 1.0 / 12.0
LOG2_E = 1.4426950408889634

X, ZH, CORE, Y, ZL = 4, 4, 2, 4, 4
HEADS = ZH * ZL
SLAB = 4096
RUN = 128
RUNS = ZH + 1
SLOTS = 2 * RUNS
KB = 256
BLOCKS = SLOTS * 512 // KB
MOST = 14
PACK_STEP = 1 << 15


def token_codes(positions, pack_table):
    starts = pack_table[:, 0]
    pack_id = jnp.sum((positions[:, None] >= starts[None, :]).astype(jnp.int32), axis=1) - 1
    chosen = pack_id[:, None] == jnp.arange(pack_table.shape[0], dtype=jnp.int32)[None, :]
    bounds = jnp.sum(jnp.where(chosen[:, :, None], pack_table[None, :, :], 0), axis=1)
    role = (positions >= bounds[:, 1]).astype(jnp.int32) + (positions >= bounds[:, 2]).astype(
        jnp.int32
    )
    logical = (
        jnp.where(role == 2, positions - bounds[:, 2] + bounds[:, 1], positions) - bounds[:, 0]
    )
    return pack_id, logical, role, bounds[:, 0]


def by_two(low, stop, step, carry):
    pairs = (stop - low) // 2

    def both(i, carry):
        return step(low + 2 * i + 1, step(low + 2 * i, carry))

    carry = lax.fori_loop(0, pairs, both, carry)
    return lax.fori_loop(low + 2 * pairs, stop, step, carry)


def slot_of(run, side):
    return 2 * run + 1 + side if run < ZH else 9 * (1 - side)


def arrange(
    where_ref, my_five, other_five, keys, values, keys_t, values_t
):
    y = where_ref[2 * RUNS]
    core = where_ref[2 * RUNS + 1]

    def place(slot, row, piece):
        block = slot * 2 + row // 2
        at = pl.multiple_of((row % 2) * RUN, RUN)
        keys[block, pl.ds(at, RUN), :] = piece[:, :HEAD_DIM]
        values[block, pl.ds(at, RUN), :] = piece[:, HEAD_DIM:]

    for dy in range(Y):
        row = (y + dy) % Y
        for run in range(RUNS):
            rows = slice(run * RUN, (run + 1) * RUN)
            place(slot_of(run, core), row, my_five[dy, rows, :])
            place(slot_of(run, 1 - core), row, other_five[dy, rows, :])

    for block in range(BLOCKS):
        keys_t[block] = keys[block].T
        values_t[block] = values[block].T


def one_run(run, source, rows, refs, dq_ref, out, ratios, expos, sums):
    where_ref, query_code_ref, key_code_ref, keys, values, keys_t, values_t = refs
    f32, b16 = jnp.float32, jnp.bfloat16
    low = where_ref[run]
    high = where_ref[RUNS + run]
    query = jnp.concatenate([source[rows, 0:128], source[rows, 128:256]], axis=0)
    grad = jnp.concatenate([source[rows, 256:384], source[rows, 384:512]], axis=0)
    query_t = query.T
    grad_t = grad.T
    query_code = query_code_ref[run : run + 1, :]

    def forward(block, carry):
        total, weighted = carry
        raw = jnp.dot(keys[block], query_t, preferred_element_type=f32)
        ratio = jnp.tanh(raw * (SCORE_SCALE / SOFT_CAP))
        expo = jnp.exp2(ratio * (SOFT_CAP * LOG2_E))
        gap = query_code - key_code_ref[pl.ds(pl.multiple_of(block * KB, KB), KB), :]
        seen = (gap >= 0) & (gap < 8 * WINDOW) & ((gap & 7) != 1)
        expo = jnp.concatenate(
            [jnp.where(seen, expo[:, :RUN], 0.0), jnp.where(seen, expo[:, RUN:], 0.0)], axis=1
        )
        ratios[block - low] = ratio
        expos[block - low] = expo
        total = total + jnp.sum(expo, axis=0, keepdims=True)
        weighted = weighted + jnp.dot(
            values_t[block], expo.astype(b16), preferred_element_type=f32
        )
        return total, weighted

    total, weighted = by_two(
        low, high + 1, forward,
        (jnp.zeros((1, 2 * RUN), f32), jnp.zeros((HEAD_DIM, 2 * RUN), f32)),
    )
    scale = jnp.where(total > 0.0, 1.0 / total, 0.0)
    delta = jnp.sum(grad_t.astype(f32) * weighted, axis=0, keepdims=True) * scale

    def backward(block, dq_t):
        ratio = ratios[block - low]
        prob = expos[block - low] * scale
        dprob = jnp.dot(values[block], grad_t, preferred_element_type=f32)
        dscore = prob * (dprob - delta) * ((1.0 - ratio * ratio) * SCORE_SCALE)
        dscore = dscore.astype(b16)
        dq_t = dq_t + jnp.dot(keys_t[block], dscore, preferred_element_type=f32)
        dk = jnp.dot(dscore, query, preferred_element_type=f32)
        dv = jnp.dot(prob.astype(b16), grad, preferred_element_type=f32)
        sums[block] = sums[block] + jnp.concatenate([dk, dv], axis=1)
        return dq_t

    dq_t = by_two(low, high + 1, backward, jnp.zeros((HEAD_DIM, 2 * RUN), f32))
    dq_ref[out, 0:128] = dq_t[:, :RUN].T.astype(b16)
    dq_ref[out, 128:256] = dq_t[:, RUN:].T.astype(b16)


def attend_tail(
    where_ref, query_code_ref, key_code_ref, keys, values, keys_t, values_t, tail_ref,
    dq_ref, sums,
    ratios, expos,
):
    refs = (where_ref, query_code_ref, key_code_ref, keys, values, keys_t, values_t)
    whole = slice(0, RUN)
    for block in range(BLOCKS):
        sums[block] = jnp.zeros((KB, 2 * HEAD_DIM), jnp.float32)
    core = where_ref[2 * RUNS + 1]

    @pl.when(core == 0)
    def _():
        one_run(ZH, tail_ref, whole, refs, dq_ref, whole, ratios, expos, sums)

    @pl.when(core != 0)
    def _():
        dq_ref[...] = jnp.zeros((RUN, 256), jnp.bfloat16)


def attend(
    where_ref, query_code_ref, key_code_ref, keys, values, keys_t, values_t, qg_ref, tail_sums,
    dq_ref, mine_ref, other_ref,
    ratios, expos, sums,
):
    y = where_ref[2 * RUNS]
    core = where_ref[2 * RUNS + 1]
    b16 = jnp.bfloat16
    refs = (where_ref, query_code_ref, key_code_ref, keys, values, keys_t, values_t)
    for block in range(BLOCKS):
        sums[block] = tail_sums[block]

    for run in range(ZH):
        rows = slice(run * RUN, (run + 1) * RUN)
        one_run(run, qg_ref, rows, refs, dq_ref, rows, ratios, expos, sums)

    for dy in range(Y):
        row = (y + dy) % Y
        at = pl.multiple_of((row % 2) * RUN, RUN)
        for run in range(RUNS):
            rows = slice(run * RUN, (run + 1) * RUN)
            mine_ref[dy, rows, :] = sums[slot_of(run, core) * 2 + row // 2, pl.ds(at, RUN), :]
            other_ref[dy, rows, :] = sums[
                slot_of(run, 1 - core) * 2 + row // 2, pl.ds(at, RUN), :
            ].astype(b16)


def call_arrange(where, pieces):
    vmem = pl.BlockSpec(memory_space=pltpu.VMEM)
    straight = jax.ShapeDtypeStruct((BLOCKS, KB, HEAD_DIM), jnp.bfloat16)
    turned = jax.ShapeDtypeStruct((BLOCKS, HEAD_DIM, KB), jnp.bfloat16)
    return pl.pallas_call(
        arrange,
        out_shape=(straight, straight, turned, turned),
        in_specs=[pl.BlockSpec(memory_space=pltpu.SMEM)] + [vmem] * 2,
        out_specs=(vmem,) * 4,
        compiler_params=pltpu.CompilerParams(vmem_limit_bytes=12 << 20),
        name="arrange",
    )(where, *pieces)


def call_tail(where, query_code, key_code, arranged, tail):
    vmem = pl.BlockSpec(memory_space=pltpu.VMEM)
    return pl.pallas_call(
        attend_tail,
        out_shape=(
            jax.ShapeDtypeStruct((RUN, 256), jnp.bfloat16),
            jax.ShapeDtypeStruct((BLOCKS, KB, 2 * HEAD_DIM), jnp.float32),
        ),
        in_specs=[pl.BlockSpec(memory_space=pltpu.SMEM)] + [vmem] * 7,
        out_specs=(vmem, vmem),
        scratch_shapes=[
            pltpu.VMEM((MOST, KB, 2 * RUN), jnp.float32),
            pltpu.VMEM((MOST, KB, 2 * RUN), jnp.float32),
        ],
        compiler_params=pltpu.CompilerParams(vmem_limit_bytes=24 << 20),
        name="attend_tail",
    )(where, query_code, key_code, *arranged, tail)


def call_attend(where, query_code, key_code, arranged, qg, tail_sums):
    vmem = pl.BlockSpec(memory_space=pltpu.VMEM)
    rows = RUNS * RUN
    return pl.pallas_call(
        attend,
        out_shape=(
            jax.ShapeDtypeStruct((ZH * RUN, 256), jnp.bfloat16),
            jax.ShapeDtypeStruct((Y, rows, 256), jnp.float32),
            jax.ShapeDtypeStruct((Y, rows, 256), jnp.bfloat16),
        ),
        in_specs=[pl.BlockSpec(memory_space=pltpu.SMEM)] + [vmem] * 8,
        out_specs=(vmem, vmem, vmem),
        scratch_shapes=[
            pltpu.VMEM((MOST, KB, 2 * RUN), jnp.float32),
            pltpu.VMEM((MOST, KB, 2 * RUN), jnp.float32),
            pltpu.VMEM((BLOCKS, KB, 2 * HEAD_DIM), jnp.float32),
        ],
        compiler_params=pltpu.CompilerParams(vmem_limit_bytes=36 << 20),
        name="attend",
    )(where, query_code, key_code, *arranged, qg, tail_sums)


def tables(x, core, y, pack_table):
    first = x * SLAB - 512
    pack, logical, role, _ = token_codes(
        first + jnp.arange(SLOTS * 512, dtype=jnp.int32), pack_table
    )
    key_code = 8 * (pack * PACK_STEP + logical) + role
    key_code = jnp.broadcast_to(key_code[:, None], (SLOTS * 512, RUN))
    runs = jnp.arange(RUNS, dtype=jnp.int32)
    tail = runs == ZH
    begin = x * SLAB + runs * 1024 + jnp.where(tail, 0, core * 512) + y * RUN
    position = begin[:, None] + jnp.arange(RUN, dtype=jnp.int32)[None, :]
    pack, logical, role, start = (
        part.reshape(RUNS, RUN) for part in token_codes(position.reshape(-1), pack_table)
    )
    home = pack // 2
    taken = jnp.where(tail[:, None], (home == x) & (core == 0), home >= x)
    taken = taken & (position < pack_table[-1, 3])
    query_code = jnp.where(taken, 8 * (pack * PACK_STEP + logical) + 4 - role, -(1 << 30))
    high = (begin - first) // KB
    low = (jnp.min(jnp.where(taken, start, 1 << 28), axis=1) - first) // KB
    low = jnp.maximum(jnp.maximum(low, high - (MOST - 1)), 0)
    some = jnp.any(taken, axis=1)
    low, high = jnp.where(some, low, 1), jnp.where(some, high, 0)
    where = jnp.concatenate([low, high, jnp.stack([y, core])])
    return where, query_code, key_code


def ring(size, by):
    return [(i, (i + by) % size) for i in range(size)]


def local(query_states, key_states, value_states, grad_out, pack_table):
    b16, f32 = jnp.bfloat16, jnp.float32
    x, core, y = lax.axis_index("x"), lax.axis_index("core"), lax.axis_index("y")
    z = ("zh", "zl")
    tokens = query_states.shape[0]
    borders = [(2 * i, 2 * i - 2) for i in range(1, X)] + [
        (2 * i + 1, 2 * i + 3) for i in range(X - 1)
    ]
    back = [(b, a) for a, b in borders]
    tails = [(2 * i, 2 * i - 2) for i in range(1, X)]

    def by_head(value):
        return jnp.transpose(value.reshape(tokens, HEADS, -1), (1, 0, 2))

    kv = jnp.concatenate([by_head(key_states), by_head(value_states)], axis=2)
    qg = jnp.concatenate([by_head(query_states), by_head(grad_out)], axis=2)
    kv = lax.all_to_all(kv, z, split_axis=0, concat_axis=0, tiled=True)
    kv = kv.reshape(ZH * RUN, 256)
    where, query_code, key_code = tables(x, core, y, pack_table)
    qg, where, query_code, key_code = lax.optimization_barrier((qg, where, query_code, key_code))
    qg = lax.all_to_all(qg, z, split_axis=0, concat_axis=0, tiled=True)
    qg = qg.reshape(ZH * RUN, 512)

    border = lax.dynamic_slice(kv, (core * (ZH - 1) * RUN, 0), (RUN, 256))
    border = lax.ppermute(border, ("x", "core"), borders)
    five = jnp.concatenate([kv, border], axis=0)
    fives = [five] + [lax.ppermute(five, "y", ring(Y, -dy)) for dy in range(1, Y)]
    stack = jnp.stack(fives)
    other_five = lax.ppermute(stack, "core", ring(CORE, 1))
    arranged = call_arrange(where, (stack, other_five))
    tail = lax.ppermute(qg[:RUN], ("x", "core"), tails)
    dq_tail, tail_sums = call_tail(where, query_code, key_code, arranged, tail)
    dq_tail = lax.ppermute(dq_tail, ("x", "core"), [(b, a) for a, b in tails])
    dq, mine, other = call_attend(where, query_code, key_code, arranged, qg, tail_sums)

    other = lax.ppermute(other, "core", ring(CORE, 1))
    dq = jnp.concatenate(
        [(dq[:RUN].astype(f32) + dq_tail.astype(f32)).astype(b16), dq[RUN:]], axis=0
    )
    dq = dq.reshape(HEADS, tokens, 256)
    dq = lax.all_to_all(dq, z, split_axis=0, concat_axis=0, tiled=True)
    grad_query = jnp.transpose(dq, (1, 0, 2)).reshape(tokens, HEADS * 256)

    part = mine + other.astype(f32)
    total = part[0]
    for dy in range(1, Y):
        total = total + lax.ppermute(part[dy].astype(b16), "y", ring(Y, dy)).astype(f32)
    border = lax.ppermute(total[ZH * RUN :].astype(b16), ("x", "core"), back).astype(f32)
    gap = (ZH - 1) * RUN
    total = total[: ZH * RUN] + jnp.where(
        core == 0, jnp.pad(border, ((0, gap), (0, 0))), jnp.pad(border, ((gap, 0), (0, 0)))
    )
    dkv = total.astype(b16).reshape(HEADS, tokens, 256)
    dkv = lax.all_to_all(dkv, z, split_axis=0, concat_axis=0, tiled=True)
    dkv = jnp.transpose(dkv, (1, 0, 2))
    grad_key = dkv[:, :, :HEAD_DIM].reshape(tokens, HEADS * HEAD_DIM)
    grad_value = dkv[:, :, HEAD_DIM:].reshape(tokens, HEADS * HEAD_DIM)
    return grad_query, grad_key, grad_value


def solution(mesh):
    axes = ("x", "zh", "core", "y", "zl")
    fine = Mesh(mesh.devices.reshape(X, ZH, CORE, Y, ZL), axes)
    spread = P(axes, None)
    return jax.shard_map(
        local,
        mesh=fine,
        in_specs=(spread, spread, spread, spread, P()),
        out_specs=(spread, spread, spread),
        check_vma=False,
    )
```

```python
import jax
import jax.numpy as jnp
from jax import lax
from jax.experimental import pallas as pl
from jax.experimental.pallas import tpu as pltpu
from jax.sharding import Mesh, PartitionSpec as P

HEAD_DIM = 128
WINDOW = 4096
SOFT_CAP = 50.0
SCORE_SCALE = 1.0 / 12.0
LOG2_E = 1.4426950408889634

X, ZH, CORE, Y, ZL = 4, 4, 2, 4, 4
HEADS = ZH * ZL
SLAB = 4096
RUN = 128
RUNS = ZH + 1
HALF = ZH // 2
SLOTS = 2 * RUNS
KB = 256
BLOCKS = SLOTS * 512 // KB
MOST = 14
PACK_STEP = 1 << 15


def token_codes(positions, pack_table):
    starts = pack_table[:, 0]
    pack_id = jnp.sum((positions[:, None] >= starts[None, :]).astype(jnp.int32), axis=1) - 1
    chosen = pack_id[:, None] == jnp.arange(pack_table.shape[0], dtype=jnp.int32)[None, :]
    bounds = jnp.sum(jnp.where(chosen[:, :, None], pack_table[None, :, :], 0), axis=1)
    role = (positions >= bounds[:, 1]).astype(jnp.int32) + (positions >= bounds[:, 2]).astype(
        jnp.int32
    )
    logical = (
        jnp.where(role == 2, positions - bounds[:, 2] + bounds[:, 1], positions) - bounds[:, 0]
    )
    return pack_id, logical, role, bounds[:, 0]


def by_two(low, stop, step, carry):
    pairs = (stop - low) // 2

    def both(i, carry):
        return step(low + 2 * i + 1, step(low + 2 * i, carry))

    carry = lax.fori_loop(0, pairs, both, carry)
    return lax.fori_loop(low + 2 * pairs, stop, step, carry)


def slot_of(run, side):
    return 2 * run + 1 + side if run < ZH else 9 * (1 - side)


def arrange(
    where_ref, my_five, other_five, keys, values, keys_t, values_t
):
    y = where_ref[2 * RUNS]
    core = where_ref[2 * RUNS + 1]

    def place(slot, row, piece):
        block = slot * 2 + row // 2
        at = pl.multiple_of((row % 2) * RUN, RUN)
        keys[block, pl.ds(at, RUN), :] = piece[:, :HEAD_DIM]
        values[block, pl.ds(at, RUN), :] = piece[:, HEAD_DIM:]

    for dy in range(Y):
        row = (y + dy) % Y
        for run in range(RUNS):
            rows = slice(run * RUN, (run + 1) * RUN)
            place(slot_of(run, core), row, my_five[dy, rows, :])
            place(slot_of(run, 1 - core), row, other_five[dy, rows, :])

    for block in range(BLOCKS):
        keys_t[block] = keys[block].T
        values_t[block] = values[block].T


def one_run(run, source, rows, refs, dq_ref, out, ratios, expos, sums):
    where_ref, query_code_ref, key_code_ref, keys, values, keys_t, values_t = refs
    f32, b16 = jnp.float32, jnp.bfloat16
    low = where_ref[run]
    high = where_ref[RUNS + run]
    query = jnp.concatenate([source[rows, 0:128], source[rows, 128:256]], axis=0)
    grad = jnp.concatenate([source[rows, 256:384], source[rows, 384:512]], axis=0)
    query_t = query.T
    grad_t = grad.T
    query_code = query_code_ref[run : run + 1, :]

    def forward(block, carry):
        total, weighted = carry
        raw = jnp.dot(keys[block], query_t, preferred_element_type=f32)
        ratio = jnp.tanh(raw * (SCORE_SCALE / SOFT_CAP))
        expo = jnp.exp2(ratio * (SOFT_CAP * LOG2_E))
        gap = query_code - key_code_ref[pl.ds(pl.multiple_of(block * KB, KB), KB), :]
        seen = (gap >= 0) & (gap < 8 * WINDOW) & ((gap & 7) != 1)
        expo = jnp.concatenate(
            [jnp.where(seen, expo[:, :RUN], 0.0), jnp.where(seen, expo[:, RUN:], 0.0)], axis=1
        )
        ratios[block - low] = ratio
        expos[block - low] = expo
        total = total + jnp.sum(expo, axis=0, keepdims=True)
        weighted = weighted + jnp.dot(
            values_t[block], expo.astype(b16), preferred_element_type=f32
        )
        return total, weighted

    total, weighted = by_two(
        low, high + 1, forward,
        (jnp.zeros((1, 2 * RUN), f32), jnp.zeros((HEAD_DIM, 2 * RUN), f32)),
    )
    scale = jnp.where(total > 0.0, 1.0 / total, 0.0)
    delta = jnp.sum(grad_t.astype(f32) * weighted, axis=0, keepdims=True) * scale

    def backward(block, dq_t):
        ratio = ratios[block - low]
        prob = expos[block - low] * scale
        dprob = jnp.dot(values[block], grad_t, preferred_element_type=f32)
        dscore = prob * (dprob - delta) * ((1.0 - ratio * ratio) * SCORE_SCALE)
        dscore = dscore.astype(b16)
        dq_t = dq_t + jnp.dot(keys_t[block], dscore, preferred_element_type=f32)
        dk = jnp.dot(dscore, query, preferred_element_type=f32)
        dv = jnp.dot(prob.astype(b16), grad, preferred_element_type=f32)
        sums[block] = sums[block] + jnp.concatenate([dk, dv], axis=1)
        return dq_t

    dq_t = by_two(low, high + 1, backward, jnp.zeros((HEAD_DIM, 2 * RUN), f32))
    dq_ref[out, 0:128] = dq_t[:, :RUN].T.astype(b16)
    dq_ref[out, 128:256] = dq_t[:, RUN:].T.astype(b16)


def attend_tail(
    where_ref, query_code_ref, key_code_ref, keys, values, keys_t, values_t, tail_ref,
    dq_ref, sums,
    ratios, expos,
):
    refs = (where_ref, query_code_ref, key_code_ref, keys, values, keys_t, values_t)
    whole = slice(0, RUN)
    for block in range(BLOCKS):
        sums[block] = jnp.zeros((KB, 2 * HEAD_DIM), jnp.float32)
    core = where_ref[2 * RUNS + 1]

    @pl.when(core == 0)
    def _():
        one_run(ZH, tail_ref, whole, refs, dq_ref, whole, ratios, expos, sums)

    @pl.when(core != 0)
    def _():
        dq_ref[...] = jnp.zeros((RUN, 256), jnp.bfloat16)


def attend_first(
    where_ref, query_code_ref, key_code_ref, keys, values, keys_t, values_t, qg_ref,
    dq_ref, sums,
    ratios, expos,
):
    refs = (where_ref, query_code_ref, key_code_ref, keys, values, keys_t, values_t)
    for block in range(BLOCKS):
        sums[block] = jnp.zeros((KB, 2 * HEAD_DIM), jnp.float32)

    for run in range(HALF):
        rows = slice(run * RUN, (run + 1) * RUN)
        one_run(run, qg_ref, rows, refs, dq_ref, rows, ratios, expos, sums)


def attend_last(
    where_ref, query_code_ref, key_code_ref, keys, values, keys_t, values_t, qg_ref,
    first_sums, tail_sums,
    dq_ref, mine_ref, other_ref,
    ratios, expos, sums,
):
    y = where_ref[2 * RUNS]
    core = where_ref[2 * RUNS + 1]
    b16 = jnp.bfloat16
    refs = (where_ref, query_code_ref, key_code_ref, keys, values, keys_t, values_t)
    for block in range(BLOCKS):
        sums[block] = first_sums[block] + tail_sums[block]

    for run in range(HALF, ZH):
        rows = slice(run * RUN, (run + 1) * RUN)
        out = slice((run - HALF) * RUN, (run - HALF + 1) * RUN)
        one_run(run, qg_ref, rows, refs, dq_ref, out, ratios, expos, sums)

    for dy in range(Y):
        row = (y + dy) % Y
        at = pl.multiple_of((row % 2) * RUN, RUN)
        for run in range(RUNS):
            rows = slice(run * RUN, (run + 1) * RUN)
            mine_ref[dy, rows, :] = sums[
                slot_of(run, core) * 2 + row // 2, pl.ds(at, RUN), :
            ].astype(b16)
            other_ref[dy, rows, :] = sums[
                slot_of(run, 1 - core) * 2 + row // 2, pl.ds(at, RUN), :
            ].astype(b16)


def call_arrange(where, pieces):
    vmem = pl.BlockSpec(memory_space=pltpu.VMEM)
    straight = jax.ShapeDtypeStruct((BLOCKS, KB, HEAD_DIM), jnp.bfloat16)
    turned = jax.ShapeDtypeStruct((BLOCKS, HEAD_DIM, KB), jnp.bfloat16)
    return pl.pallas_call(
        arrange,
        out_shape=(straight, straight, turned, turned),
        in_specs=[pl.BlockSpec(memory_space=pltpu.SMEM)] + [vmem] * 2,
        out_specs=(vmem,) * 4,
        compiler_params=pltpu.CompilerParams(vmem_limit_bytes=12 << 20),
        name="arrange",
    )(where, *pieces)


def call_runs(kernel, out_shape, operands, more_scratch, grant):
    vmem = pl.BlockSpec(memory_space=pltpu.VMEM)
    return pl.pallas_call(
        kernel,
        out_shape=out_shape,
        in_specs=[pl.BlockSpec(memory_space=pltpu.SMEM)] + [vmem] * (len(operands) - 1),
        out_specs=(vmem,) * len(out_shape),
        scratch_shapes=[
            pltpu.VMEM((MOST, KB, 2 * RUN), jnp.float32),
            pltpu.VMEM((MOST, KB, 2 * RUN), jnp.float32),
            *more_scratch,
        ],
        compiler_params=pltpu.CompilerParams(vmem_limit_bytes=grant << 20),
    )(*operands)


def tables(x, core, y, pack_table):
    first = x * SLAB - 512
    pack, logical, role, _ = token_codes(
        first + jnp.arange(SLOTS * 512, dtype=jnp.int32), pack_table
    )
    key_code = 8 * (pack * PACK_STEP + logical) + role
    key_code = jnp.broadcast_to(key_code[:, None], (SLOTS * 512, RUN))
    runs = jnp.arange(RUNS, dtype=jnp.int32)
    tail = runs == ZH
    begin = x * SLAB + runs * 1024 + jnp.where(tail, 0, core * 512) + y * RUN
    position = begin[:, None] + jnp.arange(RUN, dtype=jnp.int32)[None, :]
    pack, logical, role, start = (
        part.reshape(RUNS, RUN) for part in token_codes(position.reshape(-1), pack_table)
    )
    home = pack // 2
    taken = jnp.where(tail[:, None], (home == x) & (core == 0), home >= x)
    taken = taken & (position < pack_table[-1, 3])
    query_code = jnp.where(taken, 8 * (pack * PACK_STEP + logical) + 4 - role, -(1 << 30))
    high = (begin - first) // KB
    low = (jnp.min(jnp.where(taken, start, 1 << 28), axis=1) - first) // KB
    low = jnp.maximum(jnp.maximum(low, high - (MOST - 1)), 0)
    some = jnp.any(taken, axis=1)
    low, high = jnp.where(some, low, 1), jnp.where(some, high, 0)
    where = jnp.concatenate([low, high, jnp.stack([y, core])])
    return where, query_code, key_code


def ring(size, by):
    return [(i, (i + by) % size) for i in range(size)]


def local(query_states, key_states, value_states, grad_out, pack_table):
    b16, f32 = jnp.bfloat16, jnp.float32
    x, core, y = lax.axis_index("x"), lax.axis_index("core"), lax.axis_index("y")
    z = ("zh", "zl")
    tokens = query_states.shape[0]
    borders = [(2 * i, 2 * i - 2) for i in range(1, X)] + [
        (2 * i + 1, 2 * i + 3) for i in range(X - 1)
    ]
    back = [(b, a) for a, b in borders]
    tails = [(2 * i, 2 * i - 2) for i in range(1, X)]

    def by_head(value):
        return jnp.transpose(value.reshape(tokens, HEADS, -1), (1, 0, 2))

    kv = jnp.concatenate([by_head(key_states), by_head(value_states)], axis=2)
    qg = jnp.concatenate([by_head(query_states), by_head(grad_out)], axis=2)
    kv = lax.all_to_all(kv, z, split_axis=0, concat_axis=0, tiled=True)
    kv = kv.reshape(ZH * RUN, 256)
    where, query_code, key_code = tables(x, core, y, pack_table)
    qg, where, query_code, key_code = lax.optimization_barrier((qg, where, query_code, key_code))
    qg = lax.all_to_all(qg, z, split_axis=0, concat_axis=0, tiled=True)
    qg = qg.reshape(ZH * RUN, 512)

    border = lax.dynamic_slice(kv, (core * (ZH - 1) * RUN, 0), (RUN, 256))
    border = lax.ppermute(border, ("x", "core"), borders)
    five = jnp.concatenate([kv, border], axis=0)
    fives = [five] + [lax.ppermute(five, "y", ring(Y, -dy)) for dy in range(1, Y)]
    stack = jnp.stack(fives)
    other_five = lax.ppermute(stack, "core", ring(CORE, 1))
    arranged = call_arrange(where, (stack, other_five))
    tail = lax.ppermute(qg[:RUN], ("x", "core"), tails)
    common = (where, query_code, key_code, *arranged)
    sums_shape = (BLOCKS, KB, 2 * HEAD_DIM)
    shape = jax.ShapeDtypeStruct
    dq_first, first_sums = call_runs(
        attend_first,
        (shape((HALF * RUN, 256), b16), shape(sums_shape, f32)), (*common, qg), (), 12,
    )
    dq_tail, tail_sums = call_runs(
        attend_tail,
        (shape((RUN, 256), b16), shape(sums_shape, f32)), (*common, tail), (), 12,
    )
    dq_tail = lax.ppermute(dq_tail, ("x", "core"), [(b, a) for a, b in tails])
    dq_last, mine, other = call_runs(
        attend_last,
        (
            shape(((ZH - HALF) * RUN, 256), b16),
            shape((Y, RUNS * RUN, 256), b16),
            shape((Y, RUNS * RUN, 256), b16),
        ),
        (*common, qg, first_sums, tail_sums), (pltpu.VMEM(sums_shape, f32),), 18,
    )

    other = lax.ppermute(other, "core", ring(CORE, 1))
    dq_home = (dq_first[:RUN].astype(f32) + dq_tail.astype(f32)).astype(b16)
    dq = jnp.concatenate([dq_home, dq_first[RUN:], dq_last], axis=0)
    dq = dq.reshape(HEADS, tokens, 256)
    dq = lax.all_to_all(dq, z, split_axis=0, concat_axis=0, tiled=True)
    grad_query = jnp.transpose(dq, (1, 0, 2)).reshape(tokens, HEADS * 256)

    sent = (mine[1:].astype(f32) + other[1:].astype(f32)).astype(b16)
    total = mine[0].astype(f32) + other[0].astype(f32)
    for dy in range(1, Y):
        total = total + lax.ppermute(sent[dy - 1], "y", ring(Y, dy)).astype(f32)
    border = lax.ppermute(total[ZH * RUN :].astype(b16), ("x", "core"), back).astype(f32)
    gap = (ZH - 1) * RUN
    total = total[: ZH * RUN] + jnp.where(
        core == 0, jnp.pad(border, ((0, gap), (0, 0))), jnp.pad(border, ((gap, 0), (0, 0)))
    )
    dkv = total.astype(b16).reshape(HEADS, tokens, 256)
    dkv = lax.all_to_all(dkv, z, split_axis=0, concat_axis=0, tiled=True)
    dkv = jnp.transpose(dkv, (1, 0, 2))
    grad_key = dkv[:, :, :HEAD_DIM].reshape(tokens, HEADS * HEAD_DIM)
    grad_value = dkv[:, :, HEAD_DIM:].reshape(tokens, HEADS * HEAD_DIM)
    return grad_query, grad_key, grad_value


def solution(mesh):
    axes = ("x", "zh", "core", "y", "zl")
    fine = Mesh(mesh.devices.reshape(X, ZH, CORE, Y, ZL), axes)
    spread = P(axes, None)
    return jax.shard_map(
        local,
        mesh=fine,
        in_specs=(spread, spread, spread, spread, P()),
        out_specs=(spread, spread, spread),
        check_vma=False,
    )
```

```python
import jax
import jax.numpy as jnp
from jax import lax
from jax.experimental import pallas as pl
from jax.experimental.pallas import tpu as pltpu
from jax.sharding import Mesh, PartitionSpec as P

HEAD_DIM = 128
WINDOW = 4096
SOFT_CAP = 50.0
SCORE_SCALE = 1.0 / 12.0
LOG2_E = 1.4426950408889634

X, ZH, CORE, Y, ZL = 4, 4, 2, 4, 4
HEADS = ZH * ZL
SLAB = 4096
RUN = 128
RUNS = ZH + 1
HALF = ZH // 2
SLOTS = 2 * RUNS
KB = 256
BLOCKS = SLOTS * 512 // KB
MOST = 14
PACK_STEP = 1 << 15


def token_codes(positions, pack_table):
    starts = pack_table[:, 0]
    pack_id = jnp.sum((positions[:, None] >= starts[None, :]).astype(jnp.int32), axis=1) - 1
    chosen = pack_id[:, None] == jnp.arange(pack_table.shape[0], dtype=jnp.int32)[None, :]
    bounds = jnp.sum(jnp.where(chosen[:, :, None], pack_table[None, :, :], 0), axis=1)
    role = (positions >= bounds[:, 1]).astype(jnp.int32) + (positions >= bounds[:, 2]).astype(
        jnp.int32
    )
    logical = (
        jnp.where(role == 2, positions - bounds[:, 2] + bounds[:, 1], positions) - bounds[:, 0]
    )
    return pack_id, logical, role, bounds[:, 0]


def by_two(low, stop, step, carry):
    pairs = (stop - low) // 2
    carry = lax.fori_loop(
        0, pairs, lambda i, held: step((low + 2 * i, low + 2 * i + 1), held), carry
    )
    return lax.fori_loop(low + 2 * pairs, stop, lambda i, held: step((i,), held), carry)


def slot_of(run, side):
    return 2 * run + 1 + side if run < ZH else 9 * (1 - side)


def arrange(
    where_ref, my_five, other_five, keys, values, keys_t, values_t
):
    y = where_ref[2 * RUNS]
    core = where_ref[2 * RUNS + 1]

    def place(slot, row, piece):
        block = slot * 2 + row // 2
        at = pl.multiple_of((row % 2) * RUN, RUN)
        keys[block, pl.ds(at, RUN), :] = piece[:, :HEAD_DIM]
        values[block, pl.ds(at, RUN), :] = piece[:, HEAD_DIM:]

    for dy in range(Y):
        row = (y + dy) % Y
        for run in range(RUNS):
            rows = slice(run * RUN, (run + 1) * RUN)
            place(slot_of(run, core), row, my_five[dy, rows, :])
            place(slot_of(run, 1 - core), row, other_five[dy, rows, :])

    for block in range(BLOCKS):
        keys_t[block] = keys[block].T
        values_t[block] = values[block].T


def one_run(run, source, rows, refs, dq_ref, out, ratios, expos, sums):
    where_ref, query_code_ref, key_code_ref, keys, values, keys_t, values_t = refs
    f32, b16 = jnp.float32, jnp.bfloat16
    low = where_ref[run]
    high = where_ref[RUNS + run]
    query = jnp.concatenate([source[rows, 0:128], source[rows, 128:256]], axis=0)
    grad = jnp.concatenate([source[rows, 256:384], source[rows, 384:512]], axis=0)
    query_t = query.T
    grad_t = grad.T
    query_code = query_code_ref[run : run + 1, :]

    def forward(blocks, carry):
        total, weighted = carry
        raws = [jnp.dot(keys[block], query_t, preferred_element_type=f32) for block in blocks]
        for block, raw in zip(blocks, raws):
            ratio = jnp.tanh(raw * (SCORE_SCALE / SOFT_CAP))
            expo = jnp.exp2(ratio * (SOFT_CAP * LOG2_E))
            gap = query_code - key_code_ref[pl.ds(pl.multiple_of(block * KB, KB), KB), :]
            seen = ((gap & -(8 * WINDOW)) == 0) & ((gap & 7) != 1)
            expo = jnp.concatenate(
                [jnp.where(seen, expo[:, :RUN], 0.0), jnp.where(seen, expo[:, RUN:], 0.0)], axis=1
            )
            ratios[block - low] = ratio
            expos[block - low] = expo
            total = total + jnp.sum(expo, axis=0, keepdims=True)
            weighted = weighted + jnp.dot(
                values_t[block], expo.astype(b16), preferred_element_type=f32
            )
        return total, weighted

    total, weighted = by_two(
        low, high + 1, forward,
        (jnp.zeros((1, 2 * RUN), f32), jnp.zeros((HEAD_DIM, 2 * RUN), f32)),
    )
    scale = jnp.where(total > 0.0, 1.0 / total, 0.0)
    delta = jnp.sum(grad_t.astype(f32) * weighted, axis=0, keepdims=True) * scale

    def backward(blocks, dq_t):
        dprobs = [jnp.dot(values[block], grad_t, preferred_element_type=f32) for block in blocks]
        pairs = []
        for block, dprob in zip(blocks, dprobs):
            ratio = ratios[block - low]
            prob = expos[block - low] * scale
            dscore = prob * (dprob - delta) * ((1.0 - ratio * ratio) * SCORE_SCALE)
            pairs.append((block, prob.astype(b16), dscore.astype(b16)))
        for block, prob, dscore in pairs:
            dq_t = dq_t + jnp.dot(keys_t[block], dscore, preferred_element_type=f32)
            sums[block, :, :HEAD_DIM] += jnp.dot(dscore, query, preferred_element_type=f32)
            sums[block, :, HEAD_DIM:] += jnp.dot(prob, grad, preferred_element_type=f32)
        return dq_t

    dq_t = by_two(low, high + 1, backward, jnp.zeros((HEAD_DIM, 2 * RUN), f32))
    dq_ref[out, 0:128] = dq_t[:, :RUN].T.astype(b16)
    dq_ref[out, 128:256] = dq_t[:, RUN:].T.astype(b16)


def attend_tail(
    where_ref, query_code_ref, key_code_ref, keys, values, keys_t, values_t, tail_ref,
    dq_ref, sums,
    ratios, expos,
):
    refs = (where_ref, query_code_ref, key_code_ref, keys, values, keys_t, values_t)
    whole = slice(0, RUN)
    for block in range(BLOCKS):
        sums[block] = jnp.zeros((KB, 2 * HEAD_DIM), jnp.float32)
    core = where_ref[2 * RUNS + 1]

    @pl.when(core == 0)
    def _():
        one_run(ZH, tail_ref, whole, refs, dq_ref, whole, ratios, expos, sums)

    @pl.when(core != 0)
    def _():
        dq_ref[...] = jnp.zeros((RUN, 256), jnp.bfloat16)


def attend_first(
    where_ref, query_code_ref, key_code_ref, keys, values, keys_t, values_t, qg_ref,
    dq_ref, sums,
    ratios, expos,
):
    refs = (where_ref, query_code_ref, key_code_ref, keys, values, keys_t, values_t)
    for block in range(BLOCKS):
        sums[block] = jnp.zeros((KB, 2 * HEAD_DIM), jnp.float32)

    for run in range(HALF):
        rows = slice(run * RUN, (run + 1) * RUN)
        one_run(run, qg_ref, rows, refs, dq_ref, rows, ratios, expos, sums)


def attend_last(
    where_ref, query_code_ref, key_code_ref, keys, values, keys_t, values_t, qg_ref,
    first_sums, tail_sums,
    dq_ref, mine_ref, other_ref,
    ratios, expos, sums,
):
    y = where_ref[2 * RUNS]
    core = where_ref[2 * RUNS + 1]
    b16 = jnp.bfloat16
    refs = (where_ref, query_code_ref, key_code_ref, keys, values, keys_t, values_t)
    for block in range(BLOCKS):
        sums[block] = first_sums[block] + tail_sums[block]

    for run in range(HALF, ZH):
        rows = slice(run * RUN, (run + 1) * RUN)
        out = slice((run - HALF) * RUN, (run - HALF + 1) * RUN)
        one_run(run, qg_ref, rows, refs, dq_ref, out, ratios, expos, sums)

    for dy in range(Y):
        row = (y + dy) % Y
        at = pl.multiple_of((row % 2) * RUN, RUN)
        for run in range(RUNS):
            rows = slice(run * RUN, (run + 1) * RUN)
            mine_ref[dy, rows, :] = sums[
                slot_of(run, core) * 2 + row // 2, pl.ds(at, RUN), :
            ].astype(b16)
            other_ref[dy, rows, :] = sums[
                slot_of(run, 1 - core) * 2 + row // 2, pl.ds(at, RUN), :
            ].astype(b16)


def call_arrange(where, pieces):
    vmem = pl.BlockSpec(memory_space=pltpu.VMEM)
    straight = jax.ShapeDtypeStruct((BLOCKS, KB, HEAD_DIM), jnp.bfloat16)
    turned = jax.ShapeDtypeStruct((BLOCKS, HEAD_DIM, KB), jnp.bfloat16)
    return pl.pallas_call(
        arrange,
        out_shape=(straight, straight, turned, turned),
        in_specs=[pl.BlockSpec(memory_space=pltpu.SMEM)] + [vmem] * 2,
        out_specs=(vmem,) * 4,
        compiler_params=pltpu.CompilerParams(vmem_limit_bytes=12 << 20),
        name="arrange",
    )(where, *pieces)


def call_runs(kernel, out_shape, operands, more_scratch, grant):
    vmem = pl.BlockSpec(memory_space=pltpu.VMEM)
    return pl.pallas_call(
        kernel,
        out_shape=out_shape,
        in_specs=[pl.BlockSpec(memory_space=pltpu.SMEM)] + [vmem] * (len(operands) - 1),
        out_specs=(vmem,) * len(out_shape),
        scratch_shapes=[
            pltpu.VMEM((MOST, KB, 2 * RUN), jnp.float32),
            pltpu.VMEM((MOST, KB, 2 * RUN), jnp.float32),
            *more_scratch,
        ],
        compiler_params=pltpu.CompilerParams(vmem_limit_bytes=grant << 20),
    )(*operands)


def tables(x, core, y, pack_table):
    first = x * SLAB - 512
    pack, logical, role, _ = token_codes(
        first + jnp.arange(SLOTS * 512, dtype=jnp.int32), pack_table
    )
    key_code = 8 * (pack * PACK_STEP + logical) + role
    key_code = jnp.broadcast_to(key_code[:, None], (SLOTS * 512, RUN))
    runs = jnp.arange(RUNS, dtype=jnp.int32)
    tail = runs == ZH
    begin = x * SLAB + runs * 1024 + jnp.where(tail, 0, core * 512) + y * RUN
    position = begin[:, None] + jnp.arange(RUN, dtype=jnp.int32)[None, :]
    pack, logical, role, start = (
        part.reshape(RUNS, RUN) for part in token_codes(position.reshape(-1), pack_table)
    )
    home = pack // 2
    taken = jnp.where(tail[:, None], (home == x) & (core == 0), home >= x)
    taken = taken & (position < pack_table[-1, 3])
    query_code = jnp.where(taken, 8 * (pack * PACK_STEP + logical) + 4 - role, -(1 << 30))
    high = (begin - first) // KB
    low = (jnp.min(jnp.where(taken, start, 1 << 28), axis=1) - first) // KB
    low = jnp.maximum(jnp.maximum(low, high - (MOST - 1)), 0)
    some = jnp.any(taken, axis=1)
    low, high = jnp.where(some, low, 1), jnp.where(some, high, 0)
    where = jnp.concatenate([low, high, jnp.stack([y, core])])
    return where, query_code, key_code


def ring(size, by):
    return [(i, (i + by) % size) for i in range(size)]


def local(query_states, key_states, value_states, grad_out, pack_table):
    b16, f32 = jnp.bfloat16, jnp.float32
    x, core, y = lax.axis_index("x"), lax.axis_index("core"), lax.axis_index("y")
    z = ("zh", "zl")
    tokens = query_states.shape[0]
    borders = [(2 * i, 2 * i - 2) for i in range(1, X)] + [
        (2 * i + 1, 2 * i + 3) for i in range(X - 1)
    ]
    back = [(b, a) for a, b in borders]
    tails = [(2 * i, 2 * i - 2) for i in range(1, X)]

    def by_head(value):
        return jnp.transpose(value.reshape(tokens, HEADS, -1), (1, 0, 2))

    kv = jnp.concatenate([by_head(key_states), by_head(value_states)], axis=2)
    qg = jnp.concatenate([by_head(query_states), by_head(grad_out)], axis=2)
    kv = lax.all_to_all(kv, z, split_axis=0, concat_axis=0, tiled=True)
    kv = kv.reshape(ZH * RUN, 256)
    where, query_code, key_code = tables(x, core, y, pack_table)
    qg, where, query_code, key_code = lax.optimization_barrier((qg, where, query_code, key_code))
    qg = lax.all_to_all(qg, z, split_axis=0, concat_axis=0, tiled=True)
    qg = qg.reshape(ZH * RUN, 512)

    border = lax.dynamic_slice(kv, (core * (ZH - 1) * RUN, 0), (RUN, 256))
    border = lax.ppermute(border, ("x", "core"), borders)
    five = jnp.concatenate([kv, border], axis=0)
    fives = [five] + [lax.ppermute(five, "y", ring(Y, -dy)) for dy in range(1, Y)]
    stack = jnp.stack(fives)
    other_five = lax.ppermute(stack, "core", ring(CORE, 1))
    arranged = call_arrange(where, (stack, other_five))
    tail = lax.ppermute(qg[:RUN], ("x", "core"), tails)
    common = (where, query_code, key_code, *arranged)
    sums_shape = (BLOCKS, KB, 2 * HEAD_DIM)
    shape = jax.ShapeDtypeStruct
    dq_first, first_sums = call_runs(
        attend_first,
        (shape((HALF * RUN, 256), b16), shape(sums_shape, f32)), (*common, qg), (), 16,
    )
    dq_tail, tail_sums = call_runs(
        attend_tail,
        (shape((RUN, 256), b16), shape(sums_shape, f32)), (*common, tail), (), 16,
    )
    dq_tail = lax.ppermute(dq_tail, ("x", "core"), [(b, a) for a, b in tails])
    dq_last, mine, other = call_runs(
        attend_last,
        (
            shape(((ZH - HALF) * RUN, 256), b16),
            shape((Y, RUNS * RUN, 256), b16),
            shape((Y, RUNS * RUN, 256), b16),
        ),
        (*common, qg, first_sums, tail_sums), (pltpu.VMEM(sums_shape, f32),), 22,
    )

    other = lax.ppermute(other, "core", ring(CORE, 1))
    dq_home = (dq_first[:RUN].astype(f32) + dq_tail.astype(f32)).astype(b16)
    dq = jnp.concatenate([dq_home, dq_first[RUN:], dq_last], axis=0)
    dq = dq.reshape(HEADS, tokens, 256)
    dq = lax.all_to_all(dq, z, split_axis=0, concat_axis=0, tiled=True)
    grad_query = jnp.transpose(dq, (1, 0, 2)).reshape(tokens, HEADS * 256)

    sent = (mine[1:].astype(f32) + other[1:].astype(f32)).astype(b16)
    total = mine[0].astype(f32) + other[0].astype(f32)
    for dy in range(1, Y):
        total = total + lax.ppermute(sent[dy - 1], "y", ring(Y, dy)).astype(f32)
    border = lax.ppermute(total[ZH * RUN :].astype(b16), ("x", "core"), back).astype(f32)
    gap = (ZH - 1) * RUN
    total = total[: ZH * RUN] + jnp.where(
        core == 0, jnp.pad(border, ((0, gap), (0, 0))), jnp.pad(border, ((gap, 0), (0, 0)))
    )
    dkv = total.astype(b16).reshape(HEADS, tokens, 256)
    dkv = lax.all_to_all(dkv, z, split_axis=0, concat_axis=0, tiled=True)
    dkv = jnp.transpose(dkv, (1, 0, 2))
    grad_key = dkv[:, :, :HEAD_DIM].reshape(tokens, HEADS * HEAD_DIM)
    grad_value = dkv[:, :, HEAD_DIM:].reshape(tokens, HEADS * HEAD_DIM)
    return grad_query, grad_key, grad_value


def solution(mesh):
    axes = ("x", "zh", "core", "y", "zl")
    fine = Mesh(mesh.devices.reshape(X, ZH, CORE, Y, ZL), axes)
    spread = P(axes, None)
    return jax.shard_map(
        local,
        mesh=fine,
        in_specs=(spread, spread, spread, spread, P()),
        out_specs=(spread, spread, spread),
        check_vma=False,
    )
```

```python
import jax
import jax.numpy as jnp
from jax import lax
from jax.experimental import pallas as pl
from jax.experimental.pallas import tpu as pltpu
from jax.sharding import Mesh, PartitionSpec as P

HEAD_DIM = 128
WINDOW = 4096
SOFT_CAP = 50.0
SCORE_SCALE = 1.0 / 12.0
LOG2_E = 1.4426950408889634

X, ZH, CORE, Y, ZL = 4, 4, 2, 4, 4
HEADS = ZH * ZL
SLAB = 4096
RUN = 128
RUNS = ZH + 1
SLOTS = 2 * RUNS
KB = 256
BLOCKS = SLOTS * 512 // KB
MOST = 14
PACK_STEP = 1 << 15


def token_codes(positions, pack_table):
    starts = pack_table[:, 0]
    pack_id = jnp.sum((positions[:, None] >= starts[None, :]).astype(jnp.int32), axis=1) - 1
    chosen = pack_id[:, None] == jnp.arange(pack_table.shape[0], dtype=jnp.int32)[None, :]
    bounds = jnp.sum(jnp.where(chosen[:, :, None], pack_table[None, :, :], 0), axis=1)
    role = (positions >= bounds[:, 1]).astype(jnp.int32) + (positions >= bounds[:, 2]).astype(
        jnp.int32
    )
    logical = (
        jnp.where(role == 2, positions - bounds[:, 2] + bounds[:, 1], positions) - bounds[:, 0]
    )
    return pack_id, logical, role, bounds[:, 0]


def by_two(low, stop, step, carry):
    pairs = (stop - low) // 2
    carry = lax.fori_loop(
        0, pairs, lambda i, held: step((low + 2 * i, low + 2 * i + 1), held), carry
    )
    return lax.fori_loop(low + 2 * pairs, stop, lambda i, held: step((i,), held), carry)


def slot_of(run, side):
    return 2 * run + 1 + side if run < ZH else 9 * (1 - side)


def arrange(
    where_ref, my_five, other_five, keys, values, keys_t, values_t
):
    y = where_ref[2 * RUNS]
    core = where_ref[2 * RUNS + 1]

    def place(slot, row, piece):
        block = slot * 2 + row // 2
        at = pl.multiple_of((row % 2) * RUN, RUN)
        keys[block, pl.ds(at, RUN), :] = piece[:, :HEAD_DIM]
        values[block, pl.ds(at, RUN), :] = piece[:, HEAD_DIM:]

    for dy in range(Y):
        row = (y + dy) % Y
        for run in range(RUNS):
            rows = slice(run * RUN, (run + 1) * RUN)
            place(slot_of(run, core), row, my_five[dy, rows, :])
            place(slot_of(run, 1 - core), row, other_five[dy, rows, :])

    for block in range(BLOCKS):
        keys_t[block] = keys[block].T
        values_t[block] = values[block].T


def one_run(run, source, rows, refs, dq_ref, out, ratios, expos, sums):
    where_ref, query_code_ref, key_code_ref, keys, values, keys_t, values_t = refs
    f32, b16 = jnp.float32, jnp.bfloat16
    low = where_ref[run]
    high = where_ref[RUNS + run]
    query = jnp.concatenate([source[rows, 0:128], source[rows, 128:256]], axis=0)
    grad = jnp.concatenate([source[rows, 256:384], source[rows, 384:512]], axis=0)
    query_t = query.T
    grad_t = grad.T
    query_code = query_code_ref[run : run + 1, :]

    def forward(blocks, carry):
        total, weighted = carry
        raws = [jnp.dot(keys[block], query_t, preferred_element_type=f32) for block in blocks]
        for block, raw in zip(blocks, raws):
            ratio = jnp.tanh(raw * (SCORE_SCALE / SOFT_CAP))
            expo = jnp.exp2(ratio * (SOFT_CAP * LOG2_E))
            gap = query_code - key_code_ref[pl.ds(pl.multiple_of(block * KB, KB), KB), :]
            seen = ((gap & -(8 * WINDOW)) == 0) & ((gap & 7) != 1)
            expo = jnp.concatenate(
                [jnp.where(seen, expo[:, :RUN], 0.0), jnp.where(seen, expo[:, RUN:], 0.0)], axis=1
            )
            ratios[block - low] = ratio
            expos[block - low] = expo
            total = total + jnp.sum(expo, axis=0, keepdims=True)
            weighted = weighted + jnp.dot(
                values_t[block], expo.astype(b16), preferred_element_type=f32
            )
        return total, weighted

    total, weighted = by_two(
        low, high + 1, forward,
        (jnp.zeros((1, 2 * RUN), f32), jnp.zeros((HEAD_DIM, 2 * RUN), f32)),
    )
    scale = jnp.where(total > 0.0, 1.0 / total, 0.0)
    delta = jnp.sum(grad_t.astype(f32) * weighted, axis=0, keepdims=True) * scale

    def backward(blocks, dq_t):
        dprobs = [jnp.dot(values[block], grad_t, preferred_element_type=f32) for block in blocks]
        pairs = []
        for block, dprob in zip(blocks, dprobs):
            ratio = ratios[block - low]
            prob = expos[block - low] * scale
            dscore = prob * (dprob - delta) * ((1.0 - ratio * ratio) * SCORE_SCALE)
            pairs.append((block, prob.astype(b16), dscore.astype(b16)))
        for block, prob, dscore in pairs:
            dq_t = dq_t + jnp.dot(keys_t[block], dscore, preferred_element_type=f32)
            sums[block, :, :HEAD_DIM] += jnp.dot(dscore, query, preferred_element_type=f32)
            sums[block, :, HEAD_DIM:] += jnp.dot(prob, grad, preferred_element_type=f32)
        return dq_t

    dq_t = by_two(low, high + 1, backward, jnp.zeros((HEAD_DIM, 2 * RUN), f32))
    dq_ref[out, 0:128] = dq_t[:, :RUN].T.astype(b16)
    dq_ref[out, 128:256] = dq_t[:, RUN:].T.astype(b16)


def attend_main(
    where_ref, query_code_ref, key_code_ref, keys, values, keys_t, values_t, qg_ref,
    dq_ref, sums,
    ratios, expos,
):
    refs = (where_ref, query_code_ref, key_code_ref, keys, values, keys_t, values_t)
    for block in range(BLOCKS):
        sums[block] = jnp.zeros((KB, 2 * HEAD_DIM), jnp.float32)

    for run in range(ZH):
        rows = slice(run * RUN, (run + 1) * RUN)
        one_run(run, qg_ref, rows, refs, dq_ref, rows, ratios, expos, sums)


def attend_tail(
    where_ref, query_code_ref, key_code_ref, keys, values, keys_t, values_t, tail_ref, main_sums,
    dq_ref, mine_ref, other_ref,
    ratios, expos, sums,
):
    y = where_ref[2 * RUNS]
    core = where_ref[2 * RUNS + 1]
    b16 = jnp.bfloat16
    refs = (where_ref, query_code_ref, key_code_ref, keys, values, keys_t, values_t)
    whole = slice(0, RUN)
    for block in range(BLOCKS):
        sums[block] = main_sums[block]

    @pl.when(core == 0)
    def _():
        one_run(ZH, tail_ref, whole, refs, dq_ref, whole, ratios, expos, sums)

    @pl.when(core != 0)
    def _():
        dq_ref[...] = jnp.zeros((RUN, 256), b16)

    for dy in range(Y):
        row = (y + dy) % Y
        at = pl.multiple_of((row % 2) * RUN, RUN)
        for run in range(RUNS):
            rows = slice(run * RUN, (run + 1) * RUN)
            mine_ref[dy, rows, :] = sums[
                slot_of(run, core) * 2 + row // 2, pl.ds(at, RUN), :
            ].astype(b16)
            other_ref[dy, rows, :] = sums[
                slot_of(run, 1 - core) * 2 + row // 2, pl.ds(at, RUN), :
            ].astype(b16)


def call_arrange(where, pieces):
    vmem = pl.BlockSpec(memory_space=pltpu.VMEM)
    straight = jax.ShapeDtypeStruct((BLOCKS, KB, HEAD_DIM), jnp.bfloat16)
    turned = jax.ShapeDtypeStruct((BLOCKS, HEAD_DIM, KB), jnp.bfloat16)
    return pl.pallas_call(
        arrange,
        out_shape=(straight, straight, turned, turned),
        in_specs=[pl.BlockSpec(memory_space=pltpu.SMEM)] + [vmem] * 2,
        out_specs=(vmem,) * 4,
        compiler_params=pltpu.CompilerParams(vmem_limit_bytes=12 << 20),
        name="arrange",
    )(where, *pieces)


def call_runs(kernel, out_shape, operands, more_scratch, grant):
    vmem = pl.BlockSpec(memory_space=pltpu.VMEM)
    return pl.pallas_call(
        kernel,
        out_shape=out_shape,
        in_specs=[pl.BlockSpec(memory_space=pltpu.SMEM)] + [vmem] * (len(operands) - 1),
        out_specs=(vmem,) * len(out_shape),
        scratch_shapes=[
            pltpu.VMEM((MOST, KB, 2 * RUN), jnp.float32),
            pltpu.VMEM((MOST, KB, 2 * RUN), jnp.float32),
            *more_scratch,
        ],
        compiler_params=pltpu.CompilerParams(vmem_limit_bytes=grant << 20),
    )(*operands)


def tables(x, core, y, pack_table):
    first = x * SLAB - 512
    pack, logical, role, _ = token_codes(
        first + jnp.arange(SLOTS * 512, dtype=jnp.int32), pack_table
    )
    key_code = 8 * (pack * PACK_STEP + logical) + role
    key_code = jnp.broadcast_to(key_code[:, None], (SLOTS * 512, RUN))
    runs = jnp.arange(RUNS, dtype=jnp.int32)
    tail = runs == ZH
    begin = x * SLAB + runs * 1024 + jnp.where(tail, 0, core * 512) + y * RUN
    position = begin[:, None] + jnp.arange(RUN, dtype=jnp.int32)[None, :]
    pack, logical, role, start = (
        part.reshape(RUNS, RUN) for part in token_codes(position.reshape(-1), pack_table)
    )
    home = pack // 2
    taken = jnp.where(tail[:, None], (home == x) & (core == 0), home >= x)
    taken = taken & (position < pack_table[-1, 3])
    query_code = jnp.where(taken, 8 * (pack * PACK_STEP + logical) + 4 - role, -(1 << 30))
    high = (begin - first) // KB
    low = (jnp.min(jnp.where(taken, start, 1 << 28), axis=1) - first) // KB
    low = jnp.maximum(jnp.maximum(low, high - (MOST - 1)), 0)
    some = jnp.any(taken, axis=1)
    low, high = jnp.where(some, low, 1), jnp.where(some, high, 0)
    where = jnp.concatenate([low, high, jnp.stack([y, core])])
    return where, query_code, key_code


def ring(size, by):
    return [(i, (i + by) % size) for i in range(size)]


def local(query_states, key_states, value_states, grad_out, pack_table):
    b16, f32 = jnp.bfloat16, jnp.float32
    x, core, y = lax.axis_index("x"), lax.axis_index("core"), lax.axis_index("y")
    z = ("zh", "zl")
    tokens = query_states.shape[0]
    borders = [(2 * i, 2 * i - 2) for i in range(1, X)] + [
        (2 * i + 1, 2 * i + 3) for i in range(X - 1)
    ]
    back = [(b, a) for a, b in borders]
    tails = [(2 * i, 2 * i - 2) for i in range(1, X)]

    def by_head(value):
        return jnp.transpose(value.reshape(tokens, HEADS, -1), (1, 0, 2))

    kv = jnp.concatenate([by_head(key_states), by_head(value_states)], axis=2)
    qg = jnp.concatenate([by_head(query_states), by_head(grad_out)], axis=2)
    kv = lax.all_to_all(kv, z, split_axis=0, concat_axis=0, tiled=True)
    kv = kv.reshape(ZH * RUN, 256)
    where, query_code, key_code = tables(x, core, y, pack_table)
    qg, where, query_code, key_code = lax.optimization_barrier((qg, where, query_code, key_code))
    qg = lax.all_to_all(qg, z, split_axis=0, concat_axis=0, tiled=True)
    qg = qg.reshape(ZH * RUN, 512)

    border = lax.dynamic_slice(kv, (core * (ZH - 1) * RUN, 0), (RUN, 256))
    border = lax.ppermute(border, ("x", "core"), borders)
    five = jnp.concatenate([kv, border], axis=0)
    fives = [five] + [lax.ppermute(five, "y", ring(Y, -dy)) for dy in range(1, Y)]
    stack = jnp.stack(fives)
    other_five = lax.ppermute(stack, "core", ring(CORE, 1))
    arranged = call_arrange(where, (stack, other_five))
    tail = lax.ppermute(qg[:RUN], ("x", "core"), tails)
    common = (where, query_code, key_code, *arranged)
    sums_shape = (BLOCKS, KB, 2 * HEAD_DIM)
    shape = jax.ShapeDtypeStruct
    dq, main_sums = call_runs(
        attend_main,
        (shape((ZH * RUN, 256), b16), shape(sums_shape, f32)), (*common, qg), (), 16,
    )
    dq_tail, mine, other = call_runs(
        attend_tail,
        (
            shape((RUN, 256), b16),
            shape((Y, RUNS * RUN, 256), b16),
            shape((Y, RUNS * RUN, 256), b16),
        ),
        (*common, tail, main_sums), (pltpu.VMEM(sums_shape, f32),), 22,
    )

    other = lax.ppermute(other, "core", ring(CORE, 1))
    dq_tail = lax.ppermute(dq_tail, ("x", "core"), [(b, a) for a, b in tails])
    dq_home = (dq[:RUN].astype(f32) + dq_tail.astype(f32)).astype(b16)
    dq = jnp.concatenate([dq_home, dq[RUN:]], axis=0)
    dq = dq.reshape(HEADS, tokens, 256)
    dq = lax.all_to_all(dq, z, split_axis=0, concat_axis=0, tiled=True)
    grad_query = jnp.transpose(dq, (1, 0, 2)).reshape(tokens, HEADS * 256)

    sent = (mine[1:].astype(f32) + other[1:].astype(f32)).astype(b16)
    total = mine[0].astype(f32) + other[0].astype(f32)
    for dy in range(1, Y):
        total = total + lax.ppermute(sent[dy - 1], "y", ring(Y, dy)).astype(f32)
    border = lax.ppermute(total[ZH * RUN :].astype(b16), ("x", "core"), back).astype(f32)
    gap = (ZH - 1) * RUN
    total = total[: ZH * RUN] + jnp.where(
        core == 0, jnp.pad(border, ((0, gap), (0, 0))), jnp.pad(border, ((gap, 0), (0, 0)))
    )
    dkv = total.astype(b16).reshape(HEADS, tokens, 256)
    dkv = lax.all_to_all(dkv, z, split_axis=0, concat_axis=0, tiled=True)
    dkv = jnp.transpose(dkv, (1, 0, 2))
    grad_key = dkv[:, :, :HEAD_DIM].reshape(tokens, HEADS * HEAD_DIM)
    grad_value = dkv[:, :, HEAD_DIM:].reshape(tokens, HEADS * HEAD_DIM)
    return grad_query, grad_key, grad_value


def solution(mesh):
    axes = ("x", "zh", "core", "y", "zl")
    fine = Mesh(mesh.devices.reshape(X, ZH, CORE, Y, ZL), axes)
    spread = P(axes, None)
    return jax.shard_map(
        local,
        mesh=fine,
        in_specs=(spread, spread, spread, spread, P()),
        out_specs=(spread, spread, spread),
        check_vma=False,
    )
```
